32 devices in a mesh: lat: 8 (over z, y), lon: 4 (over x, core).
Axes of the slice: x: 2, y: 2, z: 4, core: 2. Of those that a mesh axis runs over, the one named last changes fastest.
Arguments:
- pair_table: int32 [640], replicated, may hold values from 0 to 639, each once
- spectral: bfloat16 [640, 384, 1408], P('lat', 'lon'), may hold values from -0.071777344 to 0.071777344
- lat_basis: bfloat16 [640, 32, 1408], P('lat'), may hold values from -0.15625 to 0.15625
- in_weight: bfloat16 [192, 512], replicated, may hold values from -0.4375 to 0.4375
- in_bias: float32 [512], replicated, may hold values from -3 to 3
- out_weight: bfloat16 [512, 192], replicated, may hold values from -0.25 to 0.25
- out_bias: float32 [192], replicated, may hold values from -3 to 3
- cotangent: bfloat16 [64, 192, 2560], P('lat', None, 'lon'), may hold values from -0.08984375 to 0.08984375
Outputs:
- tendency: bfloat16 [64, 192, 2560], P('lat', None, 'lon')
- spectral_grad: bfloat16 [640, 384, 1408], P('lat', 'lon')
- in_weight_grad: float32 [192, 512], replicated
- in_bias_grad: float32 [512], replicated
- out_weight_grad: float32 [512, 192], replicated
- out_bias_grad: float32 [192], replicated
The draws below stay inside these ranges and needn't reach their ends.
Inputs may be any that keep to these rules, and one draw needn't show every extreme that they name: `pair_table`: each pair number appears exactly once.
All inputs are finite; a program needn't handle non-finite values.
Results may differ from the reference program's by a relative error of at most 0.015.
Values may be sent and summed in bfloat16 or wider, within the bound.
No kernel may reach another device: no remote copies, remote signals or barrier semaphores. Data moves between devices by JAX's collectives and lax.ppermute only.
A program may use at most 256 MiB of HBM per device.

```python
import math
import jax
import jax.numpy as jnp
from jax import lax

TRUNC = 1279
NLON = 2560
HID = 512
NWAVE = 1280
PAIRS = 640
PADLEN = 1408
LATW = 64
LATH = 32
CHANNELS = 192
SPECW = 384


def level_of(own_key, extent, pieces, low, high):
    loudness = 1.0
    for dim, parts in pieces:
        draws = jax.random.uniform(jax.random.fold_in(jax.random.fold_in(own_key, 6), dim), (parts,), jnp.float32, low / len(pieces), high / len(pieces))
        loudness = loudness * jnp.repeat(jnp.exp(draws), extent[dim] // parts).reshape((-1,) + (1,) * (len(extent) - 1 - dim))
    return loudness


def centred(stream_key, extent, width, most, shards=(), kind=jnp.bfloat16):
    entries = jax.random.normal(stream_key, extent, jnp.float32) * width
    if len(shards) > 0:
        entries = level_of(stream_key, extent, shards, -0.22, 0.18) * entries
    return jnp.clip(entries, min=-most, max=most).astype(kind)


def setup_inputs(seed: int = 0) -> dict:
    streams_of = jax.random.split(jax.random.key(seed), 9)
    return {
        "pair_table": jax.random.permutation(streams_of[0], PAIRS).astype(jnp.int32),
        "spectral": centred(streams_of[1], (PAIRS, SPECW, PADLEN), 0.012, 0.071777344, ((0, 8), (1, 4))),
        "lat_basis": centred(streams_of[2], (PAIRS, LATH, PADLEN), TRUNC ** -0.5, 0.15625, ((0, 8),)),
        "in_weight": centred(streams_of[3], (CHANNELS, HID), CHANNELS ** -0.5, 0.4375),
        "in_bias": centred(streams_of[4], (HID,), 0.5, 3.0, (), jnp.float32),
        "out_weight": centred(streams_of[5], (HID, CHANNELS), HID ** -0.5, 0.25),
        "out_bias": centred(streams_of[6], (CHANNELS,), 0.5, 3.0, (), jnp.float32),
        "cotangent": centred(streams_of[7], (LATW, CHANNELS, NLON), 0.015, 0.08984375, ((0, 8), (2, 4))),
    }


exact_mode = lax.Precision.HIGHEST

def rounded(value):
    return lax.optimization_barrier(value.astype(jnp.bfloat16))

def pair_masks(pair_ids, length):
    first_len = TRUNC + 1 - pair_ids
    position = jnp.arange(length, dtype=jnp.int32)[None, :]
    lower_part = position < first_len[:, None]
    upper_part = jnp.logical_and(position >= first_len[:, None], position < TRUNC + 2)
    offset = jnp.where(lower_part, position, position - first_len[:, None])
    parity = jnp.where(offset % 2 == 0, 1.0, -1.0).astype(jnp.float32)
    return (lower_part, upper_part, parity, first_len)

def wave_numbers(pair_ids):
    both = jnp.stack([pair_ids, TRUNC - pair_ids], axis=1)
    return both.reshape(-1)

def fourier_table(numbers, longitudes, lon_total):
    phase = numbers[:, None] * longitudes[None, :] % lon_total
    angle = phase.astype(jnp.float32) * (2.0 * math.pi / lon_total)
    factor = jnp.where(numbers == 0, 1.0, 2.0).astype(jnp.float32)[:, None]
    return jnp.stack([factor * jnp.cos(angle), -factor * jnp.sin(angle)], axis=1).astype(jnp.bfloat16)

def full_rows(rows_basis, signs):
    base = rows_basis.astype(jnp.float32)
    return jnp.concatenate([base, jnp.flip(base * signs[None, :], axis=0)], axis=0)

def reference(pair_table, spectral, lat_basis, in_weight, in_bias, out_weight, out_bias, cotangent):
    lower_part, upper_part, parity, first_len = pair_masks(pair_table, PADLEN)

    def synth_pair(pair_in):
        coeffs, rows_basis, low_mask, up_mask, signs = pair_in
        full = full_rows(rows_basis, signs)
        coeff_f = coeffs.astype(jnp.float32)
        empty = jnp.zeros_like(coeff_f)
        masked = jnp.stack([jnp.where(low_mask[None, :], coeff_f, empty), jnp.where(up_mask[None, :], coeff_f, empty)])
        return rounded(jnp.einsum('qkj,lj->qlk', masked, full, precision=exact_mode))
    waves = lax.map(synth_pair, (spectral, lat_basis, lower_part, upper_part, parity))
    waves = waves.reshape(NWAVE, LATW, CHANNELS, 2).astype(jnp.float32)
    numbers = wave_numbers(pair_table)
    table = fourier_table(numbers, jnp.arange(NLON, dtype=jnp.int32), NLON).astype(jnp.float32)
    grid = rounded(jnp.einsum('glkc,gcn->lkn', waves, table, precision=exact_mode))
    in_weight_f = in_weight.astype(jnp.float32)
    out_weight_f = out_weight.astype(jnp.float32)

    def column_rows(totals, rows_in):
        grid_row, cot_row = rows_in
        grid_f = grid_row.astype(jnp.float32)
        cot_f = cot_row.astype(jnp.float32)
        pre_act = jnp.einsum('kn,kh->nh', grid_f, in_weight_f, precision=exact_mode) + in_bias[None, :]
        activated, gelu_back = jax.vjp(jax.nn.gelu, pre_act)
        hidden_f = rounded(activated).astype(jnp.float32)
        tendency_row = (jnp.einsum('nh,hk->kn', hidden_f, out_weight_f, precision=exact_mode) + out_bias[:, None]).astype(jnp.bfloat16)
        hidden_grad = jnp.einsum('kn,hk->nh', cot_f, out_weight_f, precision=exact_mode)
        pre_grad = rounded(gelu_back(hidden_grad)[0]).astype(jnp.float32)
        grad_row = jnp.einsum('nh,kh->kn', pre_grad, in_weight_f, precision=exact_mode).astype(jnp.bfloat16)
        in_weight_sum, in_bias_sum, out_weight_sum, out_bias_sum = totals
        totals = (in_weight_sum + jnp.einsum('kn,nh->kh', grid_f, pre_grad, precision=exact_mode), in_bias_sum + lax.optimization_barrier(jnp.sum(pre_grad, axis=0)), out_weight_sum + jnp.einsum('nh,kn->hk', hidden_f, cot_f, precision=exact_mode), out_bias_sum + lax.optimization_barrier(jnp.sum(cot_f, axis=1)))
        return (totals, (tendency_row, grad_row))
    start_sums = (jnp.zeros((CHANNELS, HID), jnp.float32), jnp.zeros((HID,), jnp.float32), jnp.zeros((HID, CHANNELS), jnp.float32), jnp.zeros((CHANNELS,), jnp.float32))
    sums, (tendency, grid_grad) = lax.scan(column_rows, start_sums, (grid, cotangent))
    in_weight_grad, in_bias_grad, out_weight_grad, out_bias_grad = sums
    wave_grad = rounded(jnp.einsum('gcn,lkn->glkc', table, grid_grad.astype(jnp.float32), precision=exact_mode))
    wave_grad = wave_grad.reshape(PAIRS, 2, LATW, SPECW)

    def analyse_pair(pair_in):
        grads, rows_basis, low_mask, up_mask, signs = pair_in
        full = full_rows(rows_basis, signs)
        contrib = jnp.einsum('qlk,lj->qkj', grads.astype(jnp.float32), full, precision=exact_mode)
        empty = jnp.zeros_like(contrib[0])
        return (jnp.where(low_mask[None, :], contrib[0], empty) + jnp.where(up_mask[None, :], contrib[1], empty)).astype(jnp.bfloat16)
    spectral_grad = lax.map(analyse_pair, (wave_grad, lat_basis, lower_part, upper_part, parity))
    return (tendency, spectral_grad, in_weight_grad, in_bias_grad, out_weight_grad, out_bias_grad)
```

```python
import math

import jax
import jax.numpy as jnp
from jax import lax
from jax.sharding import PartitionSpec as P

TRUNC = 1279


def pair_masks(pair_ids, length):
    first_len = TRUNC + 1 - pair_ids
    position = jnp.arange(length, dtype=jnp.int32)[None, :]
    lower_part = position < first_len[:, None]
    upper_part = jnp.logical_and(position >= first_len[:, None], position < TRUNC + 2)
    offset = jnp.where(lower_part, position, position - first_len[:, None])
    parity = jnp.where(offset % 2 == 0, 1.0, -1.0).astype(jnp.float32)
    return (lower_part, upper_part, parity, first_len)


def wave_numbers(pair_ids):
    both = jnp.stack([pair_ids, TRUNC - pair_ids], axis=1)
    return both.reshape(-1)


def fourier_table(numbers, lon_total):
    step = 128 if lon_total % 128 == 0 else 1
    coarse = jnp.arange(lon_total // step, dtype=jnp.int32) * step
    fine = jnp.arange(step, dtype=jnp.int32)
    scale = 2.0 * math.pi / lon_total

    def angles(offsets):
        phase = numbers[:, None] * offsets[None, :] % lon_total
        angle = phase.astype(jnp.float32) * scale
        return jnp.cos(angle), jnp.sin(angle)

    cos_a, sin_a = angles(coarse)
    cos_b, sin_b = angles(fine)
    cos_t = cos_a[:, :, None] * cos_b[:, None, :] - sin_a[:, :, None] * sin_b[:, None, :]
    sin_t = sin_a[:, :, None] * cos_b[:, None, :] + cos_a[:, :, None] * sin_b[:, None, :]
    count = numbers.shape[0]
    factor = jnp.where(numbers == 0, 1.0, 2.0).astype(jnp.float32)[:, None]
    return jnp.stack(
        [factor * cos_t.reshape(count, lon_total), -factor * sin_t.reshape(count, lon_total)],
        axis=1,
    ).astype(jnp.bfloat16)


def per_device(
    pair_table, spectral, lat_basis, in_weight, in_bias, out_weight, out_bias, cotangent
):
    pair_dev = spectral.shape[0]
    width_local = spectral.shape[1]
    lat_half = lat_basis.shape[1]
    band_rows = cotangent.shape[0]
    block_cols = cotangent.shape[2]
    lon_total = block_cols * lax.axis_size("lon")
    first_row = lax.axis_index("lat") * pair_dev
    local_ids = lax.dynamic_slice_in_dim(pair_table, first_row, pair_dev)
    lower_part, upper_part, parity, first_len = pair_masks(local_ids, spectral.shape[2])
    rows = jnp.concatenate(
        [lat_basis, lat_basis * parity[:, None, :].astype(jnp.bfloat16)], axis=1
    )
    zero = jnp.zeros_like(rows)
    basis = jnp.stack(
        [
            jnp.where(lower_part[:, None, :], rows, zero),
            jnp.where(upper_part[:, None, :], rows, zero),
        ],
        axis=1,
    )
    lat_window = 2 * lat_half
    raw_waves = jnp.einsum(
        "pqlj,pkj->pqlk", basis, spectral, preferred_element_type=jnp.float32
    ).astype(jnp.bfloat16)
    waves = jnp.concatenate(
        [raw_waves[:, :, :lat_half], jnp.flip(raw_waves[:, :, lat_half:], axis=2)], axis=2
    )
    flat_waves = waves.reshape(2 * pair_dev, lat_window * width_local)
    band_waves = lax.all_to_all(flat_waves, "lat", split_axis=1, concat_axis=0, tiled=True)
    wave_count = band_waves.shape[0]
    coeff_grid = band_waves.reshape(wave_count, band_rows, width_local // 2, 2)
    numbers = wave_numbers(pair_table)
    full_table = fourier_table(numbers, lon_total)
    all_columns = jnp.einsum(
        "glkc,gcn->lkn", coeff_grid, full_table, preferred_element_type=jnp.float32
    ).astype(jnp.bfloat16)
    grid = lax.all_to_all(all_columns, "lon", split_axis=2, concat_axis=1, tiled=True)
    pre_act = (
        jnp.einsum("lkc,kh->lch", grid, in_weight, preferred_element_type=jnp.float32) + in_bias
    )
    activated, gelu_back = jax.vjp(jax.nn.gelu, pre_act)
    hidden = activated.astype(jnp.bfloat16)
    tendency = (
        jnp.einsum("lch,hk->lkc", hidden, out_weight, preferred_element_type=jnp.float32)
        + out_bias[None, :, None]
    ).astype(jnp.bfloat16)
    out_weight_part = jnp.einsum(
        "lch,lkc->kh", hidden, cotangent, preferred_element_type=jnp.float32
    )
    out_bias_part = jnp.sum(cotangent.astype(jnp.float32), axis=(0, 2))
    hidden_grad = jnp.einsum(
        "lkc,hk->lch", cotangent, out_weight, preferred_element_type=jnp.float32
    )
    pre_grad = gelu_back(hidden_grad)[0].astype(jnp.bfloat16)
    in_weight_part = jnp.einsum("lkc,lch->kh", grid, pre_grad, preferred_element_type=jnp.float32)
    in_bias_part = jnp.sum(pre_grad.astype(jnp.float32), axis=(0, 1))
    grid_grad = jnp.einsum(
        "lch,kh->lkc", pre_grad, in_weight, preferred_element_type=jnp.float32
    ).astype(jnp.bfloat16)
    channels, hid = in_weight.shape
    width = max(hid, channels)

    def widen(v):
        return jnp.pad(v, ((0, 0), (0, width - v.shape[1])))

    stacked = jnp.concatenate(
        [
            widen(in_weight_part),
            widen(out_weight_part),
            widen(in_bias_part[None, :]),
            widen(out_bias_part[None, :]),
        ],
        axis=0,
    )
    summed = lax.psum(stacked, ("lat", "lon"))
    in_weight_grad = summed[:channels, :hid]
    out_weight_grad = summed[channels : 2 * channels, :hid].T
    in_bias_grad = summed[2 * channels, :hid]
    out_bias_grad = summed[2 * channels + 1, :channels]
    level_rows = lax.all_to_all(grid_grad, "lon", split_axis=1, concat_axis=2, tiled=True)
    wave_grad = jnp.einsum(
        "gcn,lkn->glkc", full_table, level_rows, preferred_element_type=jnp.float32
    ).astype(jnp.bfloat16)
    flat_grad = wave_grad.reshape(wave_count, band_rows * width_local)
    pair_grad = lax.all_to_all(flat_grad, "lat", split_axis=0, concat_axis=1, tiled=True)
    pair_grad = pair_grad.reshape(pair_dev, 2, lat_window, width_local)
    pair_grad = jnp.concatenate(
        [pair_grad[:, :, :lat_half], jnp.flip(pair_grad[:, :, lat_half:], axis=2)], axis=2
    )
    spectral_grad = jnp.einsum(
        "pqlk,pqlj->pkj", pair_grad, basis, preferred_element_type=jnp.float32
    ).astype(jnp.bfloat16)
    return (tendency, spectral_grad, in_weight_grad, in_bias_grad, out_weight_grad, out_bias_grad)


def solution(mesh):
    placed = (
        P(),
        P("lat", "lon", None),
        P("lat", None, None),
        P(),
        P(),
        P(),
        P(),
        P("lat", None, "lon"),
    )
    return jax.shard_map(
        per_device,
        mesh=mesh,
        in_specs=placed,
        out_specs=(P("lat", None, "lon"), P("lat", "lon", None), P(), P(), P(), P()),
        check_vma=False,
    )
```

```python
import math

import jax
import jax.numpy as jnp
from jax import lax
from jax.experimental import pallas as pl
from jax.sharding import PartitionSpec as P

TRUNC = 1279


def pair_masks(pair_ids, length):
    first_len = TRUNC + 1 - pair_ids
    position = jnp.arange(length, dtype=jnp.int32)[None, :]
    lower_part = position < first_len[:, None]
    upper_part = jnp.logical_and(position >= first_len[:, None], position < TRUNC + 2)
    offset = jnp.where(lower_part, position, position - first_len[:, None])
    parity = jnp.where(offset % 2 == 0, 1.0, -1.0).astype(jnp.float32)
    return (lower_part, upper_part, parity, first_len)


def wave_numbers(pair_ids):
    both = jnp.stack([pair_ids, TRUNC - pair_ids], axis=1)
    return both.reshape(-1)


def table_kernel(cos_a_ref, sin_a_ref, cos_b_ref, sin_b_ref, factor_ref, out_ref):
    fine = cos_b_ref.shape[1]
    cos_b = cos_b_ref[...]
    sin_b = sin_b_ref[...]
    factor = factor_ref[...]
    for u in range(cos_a_ref.shape[1]):
        cos_a = cos_a_ref[:, u : u + 1]
        sin_a = sin_a_ref[:, u : u + 1]
        cols = slice(u * fine, (u + 1) * fine)
        out_ref[0, :, cols] = (factor * (cos_a * cos_b - sin_a * sin_b)).astype(out_ref.dtype)
        out_ref[1, :, cols] = (-factor * (sin_a * cos_b + cos_a * sin_b)).astype(out_ref.dtype)


def fourier_table(numbers, lon_total):
    fine = 128
    count = numbers.shape[0]
    coarse = jnp.arange(lon_total // fine, dtype=jnp.int32) * fine
    scale = 2.0 * math.pi / lon_total

    def angles(offsets):
        phase = numbers[:, None] * offsets[None, :] % lon_total
        angle = phase.astype(jnp.float32) * scale
        return jnp.cos(angle), jnp.sin(angle)

    cos_a, sin_a = angles(coarse)
    cos_b, sin_b = angles(jnp.arange(fine, dtype=jnp.int32))
    factor = jnp.where(numbers == 0, 1.0, 2.0).astype(jnp.float32)[:, None]
    rows = 128 if count % 128 == 0 else count
    return pl.pallas_call(
        table_kernel,
        grid=(count // rows,),
        in_specs=[
            pl.BlockSpec((rows, coarse.shape[0]), lambda i: (i, 0)),
            pl.BlockSpec((rows, coarse.shape[0]), lambda i: (i, 0)),
            pl.BlockSpec((rows, fine), lambda i: (i, 0)),
            pl.BlockSpec((rows, fine), lambda i: (i, 0)),
            pl.BlockSpec((rows, 1), lambda i: (i, 0)),
        ],
        out_specs=pl.BlockSpec((2, rows, lon_total), lambda i: (0, i, 0)),
        out_shape=jax.ShapeDtypeStruct((2, count, lon_total), jnp.bfloat16),
    )(cos_a, sin_a, cos_b, sin_b, factor)


def all_reduce(value, axes):
    count = 1
    for name in axes:
        count *= lax.axis_size(name)
    flat = value.reshape(-1)
    chunk = -(-flat.shape[0] // (count * 128)) * 128
    flat = jnp.pad(flat, (0, chunk * count - flat.shape[0]))
    parts = lax.all_to_all(flat.reshape(count, chunk), axes, 0, 0, tiled=True)
    owned = jnp.sum(parts, axis=0, keepdims=True)
    spread = jnp.broadcast_to(owned, (count, chunk))
    whole = lax.all_to_all(spread, axes, 0, 0, tiled=True).reshape(-1)
    return whole[: value.size].reshape(value.shape)


def per_device(
    pair_table, spectral, lat_basis, in_weight, in_bias, out_weight, out_bias, cotangent
):
    pair_dev = spectral.shape[0]
    width_local = spectral.shape[1]
    lat_half = lat_basis.shape[1]
    band_rows = cotangent.shape[0]
    block_cols = cotangent.shape[2]
    lon_total = block_cols * lax.axis_size("lon")
    first_row = lax.axis_index("lat") * pair_dev
    local_ids = lax.dynamic_slice_in_dim(pair_table, first_row, pair_dev)
    lower_part, upper_part, parity, first_len = pair_masks(local_ids, spectral.shape[2])
    rows = jnp.concatenate(
        [lat_basis, lat_basis * parity[:, None, :].astype(jnp.bfloat16)], axis=1
    )
    zero = jnp.zeros_like(rows)
    basis = jnp.stack(
        [
            jnp.where(lower_part[:, None, :], rows, zero),
            jnp.where(upper_part[:, None, :], rows, zero),
        ],
        axis=1,
    )
    lat_window = 2 * lat_half
    raw_waves = jnp.einsum(
        "pqlj,pkj->pqlk", basis, spectral, preferred_element_type=jnp.float32
    ).astype(jnp.bfloat16)
    waves = jnp.concatenate(
        [raw_waves[:, :, :lat_half], jnp.flip(raw_waves[:, :, lat_half:], axis=2)], axis=2
    )
    flat_waves = waves.reshape(2 * pair_dev, lat_window * width_local)
    band_waves = lax.all_to_all(flat_waves, "lat", split_axis=1, concat_axis=0, tiled=True)
    wave_count = band_waves.shape[0]
    coeff_grid = band_waves.reshape(wave_count, band_rows, width_local // 2, 2)
    numbers = wave_numbers(pair_table)
    full_table = fourier_table(numbers, lon_total)
    all_columns = jnp.einsum(
        "glkc,cgn->lkn", coeff_grid, full_table, preferred_element_type=jnp.float32
    ).astype(jnp.bfloat16)
    grid = lax.all_to_all(all_columns, "lon", split_axis=2, concat_axis=1, tiled=True)
    pre_act = (
        jnp.einsum("lkc,kh->lch", grid, in_weight, preferred_element_type=jnp.float32) + in_bias
    )
    activated, gelu_back = jax.vjp(jax.nn.gelu, pre_act)
    hidden = activated.astype(jnp.bfloat16)
    tendency = (
        jnp.einsum("lch,hk->lkc", hidden, out_weight, preferred_element_type=jnp.float32)
        + out_bias[None, :, None]
    ).astype(jnp.bfloat16)
    out_weight_part = jnp.einsum(
        "lch,lkc->kh", hidden, cotangent, preferred_element_type=jnp.float32
    )
    out_bias_part = jnp.sum(cotangent.astype(jnp.float32), axis=(0, 2))
    hidden_grad = jnp.einsum(
        "lkc,hk->lch", cotangent, out_weight, preferred_element_type=jnp.float32
    )
    pre_grad = gelu_back(hidden_grad)[0].astype(jnp.bfloat16)
    in_weight_part = jnp.einsum("lkc,lch->kh", grid, pre_grad, preferred_element_type=jnp.float32)
    in_bias_part = jnp.sum(pre_grad.astype(jnp.float32), axis=(0, 1))
    grid_grad = jnp.einsum(
        "lch,kh->lkc", pre_grad, in_weight, preferred_element_type=jnp.float32
    ).astype(jnp.bfloat16)
    channels, hid = in_weight.shape
    width = max(hid, channels)

    def widen(v):
        return jnp.pad(v, ((0, 0), (0, width - v.shape[1])))

    stacked = jnp.concatenate(
        [
            widen(in_weight_part),
            widen(out_weight_part),
            widen(in_bias_part[None, :]),
            widen(out_bias_part[None, :]),
        ],
        axis=0,
    )
    summed = all_reduce(stacked, ("lat", "lon"))
    in_weight_grad = summed[:channels, :hid]
    out_weight_grad = summed[channels : 2 * channels, :hid].T
    in_bias_grad = summed[2 * channels, :hid]
    out_bias_grad = summed[2 * channels + 1, :channels]
    level_rows = lax.all_to_all(grid_grad, "lon", split_axis=1, concat_axis=2, tiled=True)
    wave_grad = jnp.einsum(
        "cgn,lkn->glkc", full_table, level_rows, preferred_element_type=jnp.float32
    ).astype(jnp.bfloat16)
    flat_grad = wave_grad.reshape(wave_count, band_rows * width_local)
    pair_grad = lax.all_to_all(flat_grad, "lat", split_axis=0, concat_axis=1, tiled=True)
    pair_grad = pair_grad.reshape(pair_dev, 2, lat_window, width_local)
    pair_grad = jnp.concatenate(
        [pair_grad[:, :, :lat_half], jnp.flip(pair_grad[:, :, lat_half:], axis=2)], axis=2
    )
    spectral_grad = jnp.einsum(
        "pqlk,pqlj->pkj", pair_grad, basis, preferred_element_type=jnp.float32
    ).astype(jnp.bfloat16)
    return (tendency, spectral_grad, in_weight_grad, in_bias_grad, out_weight_grad, out_bias_grad)


def solution(mesh):
    placed = (
        P(),
        P("lat", "lon", None),
        P("lat", None, None),
        P(),
        P(),
        P(),
        P(),
        P("lat", None, "lon"),
    )
    return jax.shard_map(
        per_device,
        mesh=mesh,
        in_specs=placed,
        out_specs=(P("lat", None, "lon"), P("lat", "lon", None), P(), P(), P(), P()),
        check_vma=False,
    )
```

```python
import math

import jax
import jax.numpy as jnp
from jax import lax
from jax.experimental import pallas as pl
from jax.experimental.pallas import tpu as pltpu
from jax.sharding import PartitionSpec as P

TRUNC = 1279


def pair_masks(pair_ids, length):
    first_len = TRUNC + 1 - pair_ids
    position = jnp.arange(length, dtype=jnp.int32)[None, :]
    lower_part = position < first_len[:, None]
    upper_part = jnp.logical_and(position >= first_len[:, None], position < TRUNC + 2)
    offset = jnp.where(lower_part, position, position - first_len[:, None])
    parity = jnp.where(offset % 2 == 0, 1.0, -1.0).astype(jnp.float32)
    return (lower_part, upper_part, parity, first_len)


def wave_numbers(pair_ids):
    both = jnp.stack([pair_ids, TRUNC - pair_ids], axis=1)
    return both.reshape(-1)


def table_kernel(cos_a_ref, sin_a_ref, cos_b_ref, sin_b_ref, factor_ref, out_ref):
    fine = cos_b_ref.shape[1]
    cos_b = cos_b_ref[...]
    sin_b = sin_b_ref[...]
    factor = factor_ref[...]
    for u in range(cos_a_ref.shape[1]):
        cos_a = cos_a_ref[:, u : u + 1]
        sin_a = sin_a_ref[:, u : u + 1]
        cols = slice(u * fine, (u + 1) * fine)
        out_ref[0, :, cols] = (factor * (cos_a * cos_b - sin_a * sin_b)).astype(out_ref.dtype)
        out_ref[1, :, cols] = (-factor * (sin_a * cos_b + cos_a * sin_b)).astype(out_ref.dtype)


def fourier_table(numbers, lon_total):
    fine = 128
    count = numbers.shape[0]
    coarse = jnp.arange(lon_total // fine, dtype=jnp.int32) * fine
    scale = 2.0 * math.pi / lon_total

    def angles(offsets):
        phase = numbers[:, None] * offsets[None, :] % lon_total
        angle = phase.astype(jnp.float32) * scale
        return jnp.cos(angle), jnp.sin(angle)

    cos_a, sin_a = angles(coarse)
    cos_b, sin_b = angles(jnp.arange(fine, dtype=jnp.int32))
    factor = jnp.where(numbers == 0, 1.0, 2.0).astype(jnp.float32)[:, None]
    rows = 128 if count % 128 == 0 else count
    return pl.pallas_call(
        table_kernel,
        grid=(count // rows,),
        in_specs=[
            pl.BlockSpec((rows, coarse.shape[0]), lambda i: (i, 0)),
            pl.BlockSpec((rows, coarse.shape[0]), lambda i: (i, 0)),
            pl.BlockSpec((rows, fine), lambda i: (i, 0)),
            pl.BlockSpec((rows, fine), lambda i: (i, 0)),
            pl.BlockSpec((rows, 1), lambda i: (i, 0)),
        ],
        out_specs=pl.BlockSpec((2, rows, lon_total), lambda i: (0, i, 0)),
        out_shape=jax.ShapeDtypeStruct((2, count, lon_total), jnp.bfloat16),
    )(cos_a, sin_a, cos_b, sin_b, factor)


def all_reduce(value, axes):
    count = 1
    for name in axes:
        count *= lax.axis_size(name)
    flat = value.reshape(-1)
    chunk = -(-flat.shape[0] // (count * 128)) * 128
    flat = jnp.pad(flat, (0, chunk * count - flat.shape[0]))
    parts = lax.all_to_all(flat.reshape(count, chunk), axes, 0, 0, tiled=True)
    owned = jnp.sum(parts, axis=0, keepdims=True)
    spread = jnp.broadcast_to(owned, (count, chunk))
    whole = lax.all_to_all(spread, axes, 0, 0, tiled=True).reshape(-1)
    return whole[: value.size].reshape(value.shape)


def masked_rows(ids_ref, pair_index, basis, rows_ref):
    half, length = basis.shape
    pair = ids_ref[pair_index]
    first = TRUNC + 1 - pair
    position = lax.broadcasted_iota(jnp.int32, (1, length), 1)
    lower = position < first
    upper = jnp.logical_and(position >= first, position < TRUNC + 2)
    offset = jnp.where(lower, position, position - first)
    odd = offset % 2 == 1
    zero = jnp.zeros_like(basis)
    signed = jnp.where(odd, -basis, basis)
    rows_ref[0:half, :] = jnp.where(lower, basis, zero)
    rows_ref[half : 2 * half, :] = jnp.where(lower, signed, zero)
    rows_ref[2 * half : 3 * half, :] = jnp.where(upper, basis, zero)
    rows_ref[3 * half : 4 * half, :] = jnp.where(upper, signed, zero)


def synth_kernel(ids_ref, spec_ref, basis_ref, out_ref, rows_ref):
    block = basis_ref.shape[0]
    step = pl.program_id(0)
    for i in range(block):
        masked_rows(ids_ref, step * block + i, basis_ref[i], rows_ref)
        out = lax.dot_general(
            rows_ref[...], spec_ref[i], (((1,), (1,)), ((), ())),
            preferred_element_type=jnp.float32,
        )
        out_ref[i] = out.astype(out_ref.dtype)


def analyse_kernel(ids_ref, grad_ref, basis_ref, out_ref, rows_ref):
    block = basis_ref.shape[0]
    step = pl.program_id(0)
    for i in range(block):
        masked_rows(ids_ref, step * block + i, basis_ref[i], rows_ref)
        out = jnp.dot(grad_ref[i], rows_ref[...], preferred_element_type=jnp.float32)
        out_ref[i] = out.astype(out_ref.dtype)


def pair_block(count):
    for size in (8, 4, 2, 1):
        if count % size == 0:
            return size


def synthesis(local_ids, spectral, lat_basis):
    pairs, width, length = spectral.shape
    half = lat_basis.shape[1]
    block = pair_block(pairs)
    spec = pltpu.PrefetchScalarGridSpec(
        num_scalar_prefetch=1,
        grid=(pairs // block,),
        in_specs=[
            pl.BlockSpec((block, width, length), lambda s, ids: (s, 0, 0)),
            pl.BlockSpec((block, half, length), lambda s, ids: (s, 0, 0)),
        ],
        out_specs=pl.BlockSpec((block, 4 * half, width), lambda s, ids: (s, 0, 0)),
        scratch_shapes=[pltpu.VMEM((4 * half, length), lat_basis.dtype)],
    )
    return pl.pallas_call(
        synth_kernel,
        grid_spec=spec,
        out_shape=jax.ShapeDtypeStruct((pairs, 4 * half, width), jnp.bfloat16),
    )(local_ids, spectral, lat_basis)


def analysis(local_ids, grads, lat_basis):
    pairs, width, rows = grads.shape
    half, length = lat_basis.shape[1], lat_basis.shape[2]
    block = pair_block(pairs)
    spec = pltpu.PrefetchScalarGridSpec(
        num_scalar_prefetch=1,
        grid=(pairs // block,),
        in_specs=[
            pl.BlockSpec((block, width, rows), lambda s, ids: (s, 0, 0)),
            pl.BlockSpec((block, half, length), lambda s, ids: (s, 0, 0)),
        ],
        out_specs=pl.BlockSpec((block, width, length), lambda s, ids: (s, 0, 0)),
        scratch_shapes=[pltpu.VMEM((4 * half, length), lat_basis.dtype)],
    )
    return pl.pallas_call(
        analyse_kernel,
        grid_spec=spec,
        out_shape=jax.ShapeDtypeStruct((pairs, width, length), jnp.bfloat16),
    )(local_ids, grads, lat_basis)


def per_device(
    pair_table, spectral, lat_basis, in_weight, in_bias, out_weight, out_bias, cotangent
):
    pair_dev = spectral.shape[0]
    width_local = spectral.shape[1]
    lat_half = lat_basis.shape[1]
    band_rows = cotangent.shape[0]
    block_cols = cotangent.shape[2]
    lon_total = block_cols * lax.axis_size("lon")
    first_row = lax.axis_index("lat") * pair_dev
    local_ids = lax.dynamic_slice_in_dim(pair_table, first_row, pair_dev)
    lat_window = 2 * lat_half
    raw_waves = synthesis(local_ids, spectral, lat_basis).reshape(
        pair_dev, 2, lat_window, width_local
    )
    waves = jnp.concatenate(
        [raw_waves[:, :, :lat_half], jnp.flip(raw_waves[:, :, lat_half:], axis=2)], axis=2
    )
    flat_waves = waves.reshape(2 * pair_dev, lat_window * width_local)
    band_waves = lax.all_to_all(flat_waves, "lat", split_axis=1, concat_axis=0, tiled=True)
    wave_count = band_waves.shape[0]
    coeff_grid = band_waves.reshape(wave_count, band_rows, width_local // 2, 2)
    numbers = wave_numbers(pair_table)
    full_table = fourier_table(numbers, lon_total)
    all_columns = jnp.einsum(
        "glkc,cgn->lkn", coeff_grid, full_table, preferred_element_type=jnp.float32
    ).astype(jnp.bfloat16)
    grid = lax.all_to_all(all_columns, "lon", split_axis=2, concat_axis=1, tiled=True)
    pre_act = (
        jnp.einsum("lkc,kh->lch", grid, in_weight, preferred_element_type=jnp.float32) + in_bias
    )
    activated, gelu_back = jax.vjp(jax.nn.gelu, pre_act)
    hidden = activated.astype(jnp.bfloat16)
    tendency = (
        jnp.einsum("lch,hk->lkc", hidden, out_weight, preferred_element_type=jnp.float32)
        + out_bias[None, :, None]
    ).astype(jnp.bfloat16)
    out_weight_part = jnp.einsum(
        "lch,lkc->kh", hidden, cotangent, preferred_element_type=jnp.float32
    )
    out_bias_part = jnp.sum(cotangent.astype(jnp.float32), axis=(0, 2))
    hidden_grad = jnp.einsum(
        "lkc,hk->lch", cotangent, out_weight, preferred_element_type=jnp.float32
    )
    pre_grad = gelu_back(hidden_grad)[0].astype(jnp.bfloat16)
    in_weight_part = jnp.einsum("lkc,lch->kh", grid, pre_grad, preferred_element_type=jnp.float32)
    in_bias_part = jnp.sum(pre_grad.astype(jnp.float32), axis=(0, 1))
    grid_grad = jnp.einsum(
        "lch,kh->lkc", pre_grad, in_weight, preferred_element_type=jnp.float32
    ).astype(jnp.bfloat16)
    channels, hid = in_weight.shape
    width = max(hid, channels)

    def widen(v):
        return jnp.pad(v, ((0, 0), (0, width - v.shape[1])))

    stacked = jnp.concatenate(
        [
            widen(in_weight_part),
            widen(out_weight_part),
            widen(in_bias_part[None, :]),
            widen(out_bias_part[None, :]),
        ],
        axis=0,
    )
    summed = all_reduce(stacked, ("lat", "lon"))
    in_weight_grad = summed[:channels, :hid]
    out_weight_grad = summed[channels : 2 * channels, :hid].T
    in_bias_grad = summed[2 * channels, :hid]
    out_bias_grad = summed[2 * channels + 1, :channels]
    level_rows = lax.all_to_all(grid_grad, "lon", split_axis=1, concat_axis=2, tiled=True)
    wave_grad = jnp.einsum(
        "cgn,lkn->glkc", full_table, level_rows, preferred_element_type=jnp.float32
    ).astype(jnp.bfloat16)
    flat_grad = wave_grad.reshape(wave_count, band_rows * width_local)
    pair_grad = lax.all_to_all(flat_grad, "lat", split_axis=0, concat_axis=1, tiled=True)
    pair_grad = pair_grad.reshape(pair_dev, 2, lat_window, width_local)
    pair_grad = jnp.concatenate(
        [pair_grad[:, :, :lat_half], jnp.flip(pair_grad[:, :, lat_half:], axis=2)], axis=2
    )
    pair_grad = jnp.swapaxes(pair_grad.reshape(pair_dev, 2 * lat_window, width_local), 1, 2)
    spectral_grad = analysis(local_ids, pair_grad, lat_basis)
    return (tendency, spectral_grad, in_weight_grad, in_bias_grad, out_weight_grad, out_bias_grad)


def solution(mesh):
    placed = (
        P(),
        P("lat", "lon", None),
        P("lat", None, None),
        P(),
        P(),
        P(),
        P(),
        P("lat", None, "lon"),
    )
    return jax.shard_map(
        per_device,
        mesh=mesh,
        in_specs=placed,
        out_specs=(P("lat", None, "lon"), P("lat", "lon", None), P(), P(), P(), P()),
        check_vma=False,
    )
```

```python
import math

import jax
import jax.numpy as jnp
from jax import lax
from jax.experimental import pallas as pl
from jax.experimental.pallas import tpu as pltpu
from jax.sharding import PartitionSpec as P

TRUNC = 1279


def pair_masks(pair_ids, length):
    first_len = TRUNC + 1 - pair_ids
    position = jnp.arange(length, dtype=jnp.int32)[None, :]
    lower_part = position < first_len[:, None]
    upper_part = jnp.logical_and(position >= first_len[:, None], position < TRUNC + 2)
    offset = jnp.where(lower_part, position, position - first_len[:, None])
    parity = jnp.where(offset % 2 == 0, 1.0, -1.0).astype(jnp.float32)
    return (lower_part, upper_part, parity, first_len)


def wave_numbers(pair_ids):
    both = jnp.stack([pair_ids, TRUNC - pair_ids], axis=1)
    return both.reshape(-1)


def table_kernel(cos_a_ref, sin_a_ref, cos_b_ref, sin_b_ref, factor_ref, out_ref):
    fine = cos_b_ref.shape[1]
    cos_b = cos_b_ref[...]
    sin_b = sin_b_ref[...]
    factor = factor_ref[...]
    for u in range(cos_a_ref.shape[1]):
        cos_a = cos_a_ref[:, u : u + 1]
        sin_a = sin_a_ref[:, u : u + 1]
        cols = slice(u * fine, (u + 1) * fine)
        out_ref[0, :, cols] = (factor * (cos_a * cos_b - sin_a * sin_b)).astype(out_ref.dtype)
        out_ref[1, :, cols] = (-factor * (sin_a * cos_b + cos_a * sin_b)).astype(out_ref.dtype)


def fourier_table(numbers, lon_total):
    fine = 128
    count = numbers.shape[0]
    coarse = jnp.arange(lon_total // fine, dtype=jnp.int32) * fine
    scale = 2.0 * math.pi / lon_total

    def angles(offsets):
        phase = numbers[:, None] * offsets[None, :] % lon_total
        angle = phase.astype(jnp.float32) * scale
        return jnp.cos(angle), jnp.sin(angle)

    cos_a, sin_a = angles(coarse)
    cos_b, sin_b = angles(jnp.arange(fine, dtype=jnp.int32))
    factor = jnp.where(numbers == 0, 1.0, 2.0).astype(jnp.float32)[:, None]
    rows = 128 if count % 128 == 0 else count
    return pl.pallas_call(
        table_kernel,
        grid=(count // rows,),
        in_specs=[
            pl.BlockSpec((rows, coarse.shape[0]), lambda i: (i, 0)),
            pl.BlockSpec((rows, coarse.shape[0]), lambda i: (i, 0)),
            pl.BlockSpec((rows, fine), lambda i: (i, 0)),
            pl.BlockSpec((rows, fine), lambda i: (i, 0)),
            pl.BlockSpec((rows, 1), lambda i: (i, 0)),
        ],
        out_specs=pl.BlockSpec((2, rows, lon_total), lambda i: (0, i, 0)),
        out_shape=jax.ShapeDtypeStruct((2, count, lon_total), jnp.bfloat16),
    )(cos_a, sin_a, cos_b, sin_b, factor)


def all_reduce(value, axes):
    count = 1
    for name in axes:
        count *= lax.axis_size(name)
    flat = value.reshape(-1)
    chunk = -(-flat.shape[0] // (count * 128)) * 128
    flat = jnp.pad(flat, (0, chunk * count - flat.shape[0]))
    parts = lax.all_to_all(flat.reshape(count, chunk), axes, 0, 0, tiled=True)
    owned = jnp.sum(parts, axis=0, keepdims=True)
    spread = jnp.broadcast_to(owned, (count, chunk))
    whole = lax.all_to_all(spread, axes, 0, 0, tiled=True).reshape(-1)
    return whole[: value.size].reshape(value.shape)


def masked_rows(ids_ref, pair_index, basis, rows_ref):
    half, length = basis.shape
    pair = ids_ref[pair_index]
    first = TRUNC + 1 - pair
    position = lax.broadcasted_iota(jnp.int32, (1, length), 1)
    lower = position < first
    upper = jnp.logical_and(position >= first, position < TRUNC + 2)
    offset = jnp.where(lower, position, position - first)
    odd = offset % 2 == 1
    row = lax.broadcasted_iota(jnp.int32, (half, half), 0)
    col = lax.broadcasted_iota(jnp.int32, (half, half), 1)
    reverse = jnp.where(row + col == half - 1, 1.0, 0.0).astype(basis.dtype)
    mirrored = jnp.dot(reverse, basis, preferred_element_type=jnp.float32).astype(basis.dtype)
    zero = jnp.zeros_like(basis)
    signed = jnp.where(odd, -mirrored, mirrored)
    rows_ref[0:half, :] = jnp.where(lower, basis, zero)
    rows_ref[half : 2 * half, :] = jnp.where(lower, signed, zero)
    rows_ref[2 * half : 3 * half, :] = jnp.where(upper, basis, zero)
    rows_ref[3 * half : 4 * half, :] = jnp.where(upper, signed, zero)


def synth_kernel(ids_ref, spec_ref, basis_ref, out_ref, rows_ref):
    block = basis_ref.shape[0]
    step = pl.program_id(0)
    for i in range(block):
        masked_rows(ids_ref, step * block + i, basis_ref[i], rows_ref)
        out = lax.dot_general(
            rows_ref[...], spec_ref[i], (((1,), (1,)), ((), ())),
            preferred_element_type=jnp.float32,
        )
        out_ref[i] = out.astype(out_ref.dtype)


def analyse_kernel(ids_ref, grad_ref, basis_ref, out_ref, rows_ref):
    block = basis_ref.shape[0]
    step = pl.program_id(0)
    for i in range(block):
        masked_rows(ids_ref, step * block + i, basis_ref[i], rows_ref)
        out = jnp.dot(grad_ref[i], rows_ref[...], preferred_element_type=jnp.float32)
        out_ref[i] = out.astype(out_ref.dtype)


def pair_block(count):
    for size in (8, 4, 2, 1):
        if count % size == 0:
            return size


def synthesis(local_ids, spectral, lat_basis):
    pairs, width, length = spectral.shape
    half = lat_basis.shape[1]
    block = pair_block(pairs)
    spec = pltpu.PrefetchScalarGridSpec(
        num_scalar_prefetch=1,
        grid=(pairs // block,),
        in_specs=[
            pl.BlockSpec((block, width, length), lambda s, ids: (s, 0, 0)),
            pl.BlockSpec((block, half, length), lambda s, ids: (s, 0, 0)),
        ],
        out_specs=pl.BlockSpec((block, 4 * half, width), lambda s, ids: (s, 0, 0)),
        scratch_shapes=[pltpu.VMEM((4 * half, length), lat_basis.dtype)],
    )
    return pl.pallas_call(
        synth_kernel,
        grid_spec=spec,
        out_shape=jax.ShapeDtypeStruct((pairs, 4 * half, width), jnp.bfloat16),
    )(local_ids, spectral, lat_basis)


def analysis(local_ids, grads, lat_basis):
    pairs, width, rows = grads.shape
    half, length = lat_basis.shape[1], lat_basis.shape[2]
    block = pair_block(pairs)
    spec = pltpu.PrefetchScalarGridSpec(
        num_scalar_prefetch=1,
        grid=(pairs // block,),
        in_specs=[
            pl.BlockSpec((block, width, rows), lambda s, ids: (s, 0, 0)),
            pl.BlockSpec((block, half, length), lambda s, ids: (s, 0, 0)),
        ],
        out_specs=pl.BlockSpec((block, width, length), lambda s, ids: (s, 0, 0)),
        scratch_shapes=[pltpu.VMEM((4 * half, length), lat_basis.dtype)],
    )
    return pl.pallas_call(
        analyse_kernel,
        grid_spec=spec,
        out_shape=jax.ShapeDtypeStruct((pairs, width, length), jnp.bfloat16),
    )(local_ids, grads, lat_basis)


def per_device(
    pair_table, spectral, lat_basis, in_weight, in_bias, out_weight, out_bias, cotangent
):
    pair_dev = spectral.shape[0]
    width_local = spectral.shape[1]
    lat_half = lat_basis.shape[1]
    band_rows = cotangent.shape[0]
    block_cols = cotangent.shape[2]
    lon_total = block_cols * lax.axis_size("lon")
    first_row = lax.axis_index("lat") * pair_dev
    local_ids = lax.dynamic_slice_in_dim(pair_table, first_row, pair_dev)
    lat_window = 2 * lat_half
    waves = synthesis(local_ids, spectral, lat_basis).reshape(
        pair_dev, 2, lat_window, width_local
    )
    flat_waves = waves.reshape(2 * pair_dev, lat_window * width_local)
    band_waves = lax.all_to_all(flat_waves, "lat", split_axis=1, concat_axis=0, tiled=True)
    wave_count = band_waves.shape[0]
    coeff_grid = band_waves.reshape(wave_count, band_rows, width_local // 2, 2)
    numbers = wave_numbers(pair_table)
    full_table = fourier_table(numbers, lon_total)
    all_columns = jnp.einsum(
        "glkc,cgn->lkn", coeff_grid, full_table, preferred_element_type=jnp.float32
    ).astype(jnp.bfloat16)
    grid = lax.all_to_all(all_columns, "lon", split_axis=2, concat_axis=1, tiled=True)
    pre_act = (
        jnp.einsum("lkc,kh->lch", grid, in_weight, preferred_element_type=jnp.float32) + in_bias
    )
    activated, gelu_back = jax.vjp(jax.nn.gelu, pre_act)
    hidden = activated.astype(jnp.bfloat16)
    tendency = (
        jnp.einsum("lch,hk->lkc", hidden, out_weight, preferred_element_type=jnp.float32)
        + out_bias[None, :, None]
    ).astype(jnp.bfloat16)
    out_weight_part = jnp.einsum(
        "lch,lkc->kh", hidden, cotangent, preferred_element_type=jnp.float32
    )
    out_bias_part = jnp.sum(cotangent.astype(jnp.float32), axis=(0, 2))
    hidden_grad = jnp.einsum(
        "lkc,hk->lch", cotangent, out_weight, preferred_element_type=jnp.float32
    )
    pre_grad = gelu_back(hidden_grad)[0].astype(jnp.bfloat16)
    in_weight_part = jnp.einsum("lkc,lch->kh", grid, pre_grad, preferred_element_type=jnp.float32)
    in_bias_part = jnp.sum(pre_grad.astype(jnp.float32), axis=(0, 1))
    grid_grad = jnp.einsum(
        "lch,kh->lkc", pre_grad, in_weight, preferred_element_type=jnp.float32
    ).astype(jnp.bfloat16)
    channels, hid = in_weight.shape
    width = max(hid, channels)

    def widen(v):
        return jnp.pad(v, ((0, 0), (0, width - v.shape[1])))

    stacked = jnp.concatenate(
        [
            widen(in_weight_part),
            widen(out_weight_part),
            widen(in_bias_part[None, :]),
            widen(out_bias_part[None, :]),
        ],
        axis=0,
    )
    level_rows = lax.all_to_all(grid_grad, "lon", split_axis=1, concat_axis=2, tiled=True)
    wave_grad = jnp.einsum(
        "cgn,lkn->glkc", full_table, level_rows, preferred_element_type=jnp.float32
    ).astype(jnp.bfloat16)
    flat_grad = wave_grad.reshape(wave_count, band_rows * width_local)
    pair_grad = lax.all_to_all(flat_grad, "lat", split_axis=0, concat_axis=1, tiled=True)
    stacked, pair_grad = lax.optimization_barrier((stacked, pair_grad))
    pair_grad = jnp.swapaxes(pair_grad.reshape(pair_dev, 2 * lat_window, width_local), 1, 2)
    spectral_grad = analysis(local_ids, pair_grad, lat_basis)
    summed = all_reduce(stacked, ("lat", "lon"))
    in_weight_grad = summed[:channels, :hid]
    out_weight_grad = summed[channels : 2 * channels, :hid].T
    in_bias_grad = summed[2 * channels, :hid]
    out_bias_grad = summed[2 * channels + 1, :channels]
    return (tendency, spectral_grad, in_weight_grad, in_bias_grad, out_weight_grad, out_bias_grad)


def solution(mesh):
    placed = (
        P(),
        P("lat", "lon", None),
        P("lat", None, None),
        P(),
        P(),
        P(),
        P(),
        P("lat", None, "lon"),
    )
    return jax.shard_map(
        per_device,
        mesh=mesh,
        in_specs=placed,
        out_specs=(P("lat", None, "lon"), P("lat", "lon", None), P(), P(), P(), P()),
        check_vma=False,
    )
```

```python
import math

import jax
import jax.numpy as jnp
from jax import lax
from jax.experimental import pallas as pl
from jax.experimental.pallas import tpu as pltpu
from jax.sharding import PartitionSpec as P

TRUNC = 1279


def pair_masks(pair_ids, length):
    first_len = TRUNC + 1 - pair_ids
    position = jnp.arange(length, dtype=jnp.int32)[None, :]
    lower_part = position < first_len[:, None]
    upper_part = jnp.logical_and(position >= first_len[:, None], position < TRUNC + 2)
    offset = jnp.where(lower_part, position, position - first_len[:, None])
    parity = jnp.where(offset % 2 == 0, 1.0, -1.0).astype(jnp.float32)
    return (lower_part, upper_part, parity, first_len)


def wave_numbers(pair_ids):
    both = jnp.stack([pair_ids, TRUNC - pair_ids], axis=1)
    return both.reshape(-1)


def table_kernel(cos_a_ref, sin_a_ref, cos_b_ref, sin_b_ref, factor_ref, out_ref):
    fine = cos_b_ref.shape[1]
    cos_b = cos_b_ref[...]
    sin_b = sin_b_ref[...]
    factor = factor_ref[...]
    for u in range(cos_a_ref.shape[1]):
        cos_a = cos_a_ref[:, u : u + 1]
        sin_a = sin_a_ref[:, u : u + 1]
        cols = slice(u * fine, (u + 1) * fine)
        out_ref[0, :, cols] = (factor * (cos_a * cos_b - sin_a * sin_b)).astype(out_ref.dtype)
        out_ref[1, :, cols] = (-factor * (sin_a * cos_b + cos_a * sin_b)).astype(out_ref.dtype)


def fourier_table(numbers, lon_total):
    fine = 128
    count = numbers.shape[0]
    coarse = jnp.arange(lon_total // fine, dtype=jnp.int32) * fine
    scale = 2.0 * math.pi / lon_total

    def angles(offsets):
        phase = numbers[:, None] * offsets[None, :] % lon_total
        angle = phase.astype(jnp.float32) * scale
        return jnp.cos(angle), jnp.sin(angle)

    cos_a, sin_a = angles(coarse)
    cos_b, sin_b = angles(jnp.arange(fine, dtype=jnp.int32))
    factor = jnp.where(numbers == 0, 1.0, 2.0).astype(jnp.float32)[:, None]
    rows = 128 if count % 128 == 0 else count
    return pl.pallas_call(
        table_kernel,
        grid=(count // rows,),
        in_specs=[
            pl.BlockSpec((rows, coarse.shape[0]), lambda i: (i, 0)),
            pl.BlockSpec((rows, coarse.shape[0]), lambda i: (i, 0)),
            pl.BlockSpec((rows, fine), lambda i: (i, 0)),
            pl.BlockSpec((rows, fine), lambda i: (i, 0)),
            pl.BlockSpec((rows, 1), lambda i: (i, 0)),
        ],
        out_specs=pl.BlockSpec((2, rows, lon_total), lambda i: (0, i, 0)),
        out_shape=jax.ShapeDtypeStruct((2, count, lon_total), jnp.bfloat16),
    )(cos_a, sin_a, cos_b, sin_b, factor)


def all_reduce(value, axes):
    count = 1
    for name in axes:
        count *= lax.axis_size(name)
    flat = value.reshape(-1)
    chunk = -(-flat.shape[0] // (count * 128)) * 128
    flat = jnp.pad(flat, (0, chunk * count - flat.shape[0]))
    parts = lax.all_to_all(flat.reshape(count, chunk), axes, 0, 0, tiled=True)
    owned = jnp.sum(parts, axis=0, keepdims=True)
    spread = jnp.broadcast_to(owned, (count, chunk))
    whole = lax.all_to_all(spread, axes, 0, 0, tiled=True).reshape(-1)
    return whole[: value.size].reshape(value.shape)


def masked_rows(ids_ref, pair_index, basis, rows_ref):
    half, length = basis.shape
    pair = ids_ref[pair_index]
    first = TRUNC + 1 - pair
    position = lax.broadcasted_iota(jnp.int32, (1, length), 1)
    lower = position < first
    upper = jnp.logical_and(position >= first, position < TRUNC + 2)
    offset = jnp.where(lower, position, position - first)
    odd = offset % 2 == 1
    zero = jnp.zeros_like(basis)
    signed = jnp.where(odd, -basis, basis)
    rows_ref[0:half, :] = jnp.where(lower, basis, zero)
    rows_ref[half : 2 * half, :] = jnp.where(lower, signed, zero)
    rows_ref[2 * half : 3 * half, :] = jnp.where(upper, basis, zero)
    rows_ref[3 * half : 4 * half, :] = jnp.where(upper, signed, zero)


def reversal(half, dtype):
    row = lax.broadcasted_iota(jnp.int32, (half, half), 0)
    col = lax.broadcasted_iota(jnp.int32, (half, half), 1)
    return jnp.where(row + col == half - 1, 1.0, 0.0).astype(dtype)


def synth_kernel(ids_ref, spec_ref, basis_ref, out_ref, rows_ref):
    block, half = basis_ref.shape[0], basis_ref.shape[1]
    step = pl.program_id(0)
    reverse = reversal(half, out_ref.dtype)
    for i in range(block):
        masked_rows(ids_ref, step * block + i, basis_ref[i], rows_ref)
        out = lax.dot_general(
            rows_ref[...], spec_ref[i], (((1,), (1,)), ((), ())),
            preferred_element_type=jnp.float32,
        ).astype(out_ref.dtype)
        for q in range(2):
            north = slice(2 * q * half, (2 * q + 1) * half)
            south = slice((2 * q + 1) * half, (2 * q + 2) * half)
            out_ref[i, north, :] = out[north]
            out_ref[i, south, :] = jnp.dot(
                reverse, out[south], preferred_element_type=jnp.float32
            ).astype(out_ref.dtype)


def analyse_kernel(ids_ref, grad_ref, basis_ref, out_ref, rows_ref):
    block, half = basis_ref.shape[0], basis_ref.shape[1]
    step = pl.program_id(0)
    reverse = reversal(half, grad_ref.dtype)
    for i in range(block):
        masked_rows(ids_ref, step * block + i, basis_ref[i], rows_ref)
        grad = grad_ref[i]
        pieces = []
        for q in range(2):
            pieces.append(grad[:, 2 * q * half : (2 * q + 1) * half])
            south = grad[:, (2 * q + 1) * half : (2 * q + 2) * half]
            pieces.append(
                jnp.dot(south, reverse, preferred_element_type=jnp.float32).astype(grad.dtype)
            )
        grad = jnp.concatenate(pieces, axis=1)
        out = jnp.dot(grad, rows_ref[...], preferred_element_type=jnp.float32)
        out_ref[i] = out.astype(out_ref.dtype)


def pair_block(count):
    for size in (8, 4, 2, 1):
        if count % size == 0:
            return size


def synthesis(local_ids, spectral, lat_basis):
    pairs, width, length = spectral.shape
    half = lat_basis.shape[1]
    block = pair_block(pairs)
    spec = pltpu.PrefetchScalarGridSpec(
        num_scalar_prefetch=1,
        grid=(pairs // block,),
        in_specs=[
            pl.BlockSpec((block, width, length), lambda s, ids: (s, 0, 0)),
            pl.BlockSpec((block, half, length), lambda s, ids: (s, 0, 0)),
        ],
        out_specs=pl.BlockSpec((block, 4 * half, width), lambda s, ids: (s, 0, 0)),
        scratch_shapes=[pltpu.VMEM((4 * half, length), lat_basis.dtype)],
    )
    return pl.pallas_call(
        synth_kernel,
        grid_spec=spec,
        out_shape=jax.ShapeDtypeStruct((pairs, 4 * half, width), jnp.bfloat16),
    )(local_ids, spectral, lat_basis)


def analysis(local_ids, grads, lat_basis):
    pairs, width, rows = grads.shape
    half, length = lat_basis.shape[1], lat_basis.shape[2]
    block = pair_block(pairs)
    spec = pltpu.PrefetchScalarGridSpec(
        num_scalar_prefetch=1,
        grid=(pairs // block,),
        in_specs=[
            pl.BlockSpec((block, width, rows), lambda s, ids: (s, 0, 0)),
            pl.BlockSpec((block, half, length), lambda s, ids: (s, 0, 0)),
        ],
        out_specs=pl.BlockSpec((block, width, length), lambda s, ids: (s, 0, 0)),
        scratch_shapes=[pltpu.VMEM((4 * half, length), lat_basis.dtype)],
    )
    return pl.pallas_call(
        analyse_kernel,
        grid_spec=spec,
        out_shape=jax.ShapeDtypeStruct((pairs, width, length), jnp.bfloat16),
    )(local_ids, grads, lat_basis)


def per_device(
    pair_table, spectral, lat_basis, in_weight, in_bias, out_weight, out_bias, cotangent
):
    pair_dev = spectral.shape[0]
    width_local = spectral.shape[1]
    lat_half = lat_basis.shape[1]
    band_rows = cotangent.shape[0]
    block_cols = cotangent.shape[2]
    lon_total = block_cols * lax.axis_size("lon")
    first_row = lax.axis_index("lat") * pair_dev
    local_ids = lax.dynamic_slice_in_dim(pair_table, first_row, pair_dev)
    lat_window = 2 * lat_half
    waves = synthesis(local_ids, spectral, lat_basis).reshape(
        pair_dev, 2, lat_window, width_local
    )
    flat_waves = waves.reshape(2 * pair_dev, lat_window * width_local)
    band_waves = lax.all_to_all(flat_waves, "lat", split_axis=1, concat_axis=0, tiled=True)
    wave_count = band_waves.shape[0]
    coeff_grid = band_waves.reshape(wave_count, band_rows, width_local // 2, 2)
    numbers = wave_numbers(pair_table)
    full_table = fourier_table(numbers, lon_total)
    all_columns = jnp.einsum(
        "glkc,cgn->lkn", coeff_grid, full_table, preferred_element_type=jnp.float32
    ).astype(jnp.bfloat16)
    grid = lax.all_to_all(all_columns, "lon", split_axis=2, concat_axis=1, tiled=True)
    pre_act = (
        jnp.einsum("lkc,kh->lch", grid, in_weight, preferred_element_type=jnp.float32) + in_bias
    )
    activated, gelu_back = jax.vjp(jax.nn.gelu, pre_act)
    hidden = activated.astype(jnp.bfloat16)
    tendency = (
        jnp.einsum("lch,hk->lkc", hidden, out_weight, preferred_element_type=jnp.float32)
        + out_bias[None, :, None]
    ).astype(jnp.bfloat16)
    out_weight_part = jnp.einsum(
        "lch,lkc->kh", hidden, cotangent, preferred_element_type=jnp.float32
    )
    out_bias_part = jnp.sum(cotangent.astype(jnp.float32), axis=(0, 2))
    hidden_grad = jnp.einsum(
        "lkc,hk->lch", cotangent, out_weight, preferred_element_type=jnp.float32
    )
    pre_grad = gelu_back(hidden_grad)[0].astype(jnp.bfloat16)
    in_weight_part = jnp.einsum("lkc,lch->kh", grid, pre_grad, preferred_element_type=jnp.float32)
    in_bias_part = jnp.sum(pre_grad.astype(jnp.float32), axis=(0, 1))
    grid_grad = jnp.einsum(
        "lch,kh->lkc", pre_grad, in_weight, preferred_element_type=jnp.float32
    ).astype(jnp.bfloat16)
    channels, hid = in_weight.shape
    width = max(hid, channels)

    def widen(v):
        return jnp.pad(v, ((0, 0), (0, width - v.shape[1])))

    stacked = jnp.concatenate(
        [
            widen(in_weight_part),
            widen(out_weight_part),
            widen(in_bias_part[None, :]),
            widen(out_bias_part[None, :]),
        ],
        axis=0,
    )
    summed = all_reduce(stacked, ("lat", "lon"))
    in_weight_grad = summed[:channels, :hid]
    out_weight_grad = summed[channels : 2 * channels, :hid].T
    in_bias_grad = summed[2 * channels, :hid]
    out_bias_grad = summed[2 * channels + 1, :channels]
    level_rows = lax.all_to_all(grid_grad, "lon", split_axis=1, concat_axis=2, tiled=True)
    wave_grad = jnp.einsum(
        "cgn,lkn->glkc", full_table, level_rows, preferred_element_type=jnp.float32
    ).astype(jnp.bfloat16)
    flat_grad = wave_grad.reshape(wave_count, band_rows * width_local)
    pair_grad = lax.all_to_all(flat_grad, "lat", split_axis=0, concat_axis=1, tiled=True)
    pair_grad = pair_grad.reshape(pair_dev, 2, lat_window, width_local)
    pair_grad = jnp.swapaxes(pair_grad.reshape(pair_dev, 2 * lat_window, width_local), 1, 2)
    spectral_grad = analysis(local_ids, pair_grad, lat_basis)
    return (tendency, spectral_grad, in_weight_grad, in_bias_grad, out_weight_grad, out_bias_grad)


def solution(mesh):
    placed = (
        P(),
        P("lat", "lon", None),
        P("lat", None, None),
        P(),
        P(),
        P(),
        P(),
        P("lat", None, "lon"),
    )
    return jax.shard_map(
        per_device,
        mesh=mesh,
        in_specs=placed,
        out_specs=(P("lat", None, "lon"), P("lat", "lon", None), P(), P(), P(), P()),
        check_vma=False,
    )
```

```python
import math

import jax
import jax.numpy as jnp
from jax import lax
from jax.experimental import pallas as pl
from jax.experimental.pallas import tpu as pltpu
from jax.sharding import PartitionSpec as P

TRUNC = 1279


def pair_masks(pair_ids, length):
    first_len = TRUNC + 1 - pair_ids
    position = jnp.arange(length, dtype=jnp.int32)[None, :]
    lower_part = position < first_len[:, None]
    upper_part = jnp.logical_and(position >= first_len[:, None], position < TRUNC + 2)
    offset = jnp.where(lower_part, position, position - first_len[:, None])
    parity = jnp.where(offset % 2 == 0, 1.0, -1.0).astype(jnp.float32)
    return (lower_part, upper_part, parity, first_len)


def wave_numbers(pair_ids):
    both = jnp.stack([pair_ids, TRUNC - pair_ids], axis=1)
    return both.reshape(-1)


def table_kernel(cos_a_ref, sin_a_ref, cos_b_ref, sin_b_ref, factor_ref, out_ref):
    fine = cos_b_ref.shape[1]
    cos_b = cos_b_ref[...]
    sin_b = sin_b_ref[...]
    factor = factor_ref[...]
    for u in range(cos_a_ref.shape[1]):
        cos_a = cos_a_ref[:, u : u + 1]
        sin_a = sin_a_ref[:, u : u + 1]
        cols = slice(u * fine, (u + 1) * fine)
        out_ref[0, :, cols] = (factor * (cos_a * cos_b - sin_a * sin_b)).astype(out_ref.dtype)
        out_ref[1, :, cols] = (-factor * (sin_a * cos_b + cos_a * sin_b)).astype(out_ref.dtype)


def fourier_table(numbers, lon_total):
    fine = 128
    count = numbers.shape[0]
    coarse = jnp.arange(lon_total // fine, dtype=jnp.int32) * fine
    scale = 2.0 * math.pi / lon_total

    def angles(offsets):
        phase = numbers[:, None] * offsets[None, :] % lon_total
        angle = phase.astype(jnp.float32) * scale
        return jnp.cos(angle), jnp.sin(angle)

    cos_a, sin_a = angles(coarse)
    cos_b, sin_b = angles(jnp.arange(fine, dtype=jnp.int32))
    factor = jnp.where(numbers == 0, 1.0, 2.0).astype(jnp.float32)[:, None]
    rows = 128 if count % 128 == 0 else count
    return pl.pallas_call(
        table_kernel,
        grid=(count // rows,),
        in_specs=[
            pl.BlockSpec((rows, coarse.shape[0]), lambda i: (i, 0)),
            pl.BlockSpec((rows, coarse.shape[0]), lambda i: (i, 0)),
            pl.BlockSpec((rows, fine), lambda i: (i, 0)),
            pl.BlockSpec((rows, fine), lambda i: (i, 0)),
            pl.BlockSpec((rows, 1), lambda i: (i, 0)),
        ],
        out_specs=pl.BlockSpec((2, rows, lon_total), lambda i: (0, i, 0)),
        out_shape=jax.ShapeDtypeStruct((2, count, lon_total), jnp.bfloat16),
    )(cos_a, sin_a, cos_b, sin_b, factor)


def all_reduce(value, axes):
    count = 1
    for name in axes:
        count *= lax.axis_size(name)
    flat = value.reshape(-1)
    chunk = -(-flat.shape[0] // (count * 128)) * 128
    flat = jnp.pad(flat, (0, chunk * count - flat.shape[0]))
    parts = lax.all_to_all(flat.reshape(count, chunk), axes, 0, 0, tiled=True)
    owned = jnp.sum(parts, axis=0, keepdims=True)
    spread = jnp.broadcast_to(owned, (count, chunk))
    whole = lax.all_to_all(spread, axes, 0, 0, tiled=True).reshape(-1)
    return whole[: value.size].reshape(value.shape)


def masked_rows(ids_ref, pair_index, basis, rows_ref):
    half, length = basis.shape
    pair = ids_ref[pair_index]
    first = TRUNC + 1 - pair
    position = lax.broadcasted_iota(jnp.int32, (1, length), 1)
    lower = position < first
    upper = jnp.logical_and(position >= first, position < TRUNC + 2)
    offset = jnp.where(lower, position, position - first)
    odd = offset % 2 == 1
    zero = jnp.zeros_like(basis)
    signed = jnp.where(odd, -basis, basis)
    rows_ref[0:half, :] = jnp.where(lower, basis, zero)
    rows_ref[half : 2 * half, :] = jnp.where(lower, signed, zero)
    rows_ref[2 * half : 3 * half, :] = jnp.where(upper, basis, zero)
    rows_ref[3 * half : 4 * half, :] = jnp.where(upper, signed, zero)


def synth_kernel(ids_ref, spec_ref, basis_ref, out_ref, rows_ref):
    block = basis_ref.shape[0]
    step = pl.program_id(0)
    for i in range(block):
        masked_rows(ids_ref, step * block + i, basis_ref[i], rows_ref)
        out = lax.dot_general(
            rows_ref[...], spec_ref[i], (((1,), (1,)), ((), ())),
            preferred_element_type=jnp.float32,
        )
        out_ref[i] = out.astype(out_ref.dtype)


def analyse_kernel(ids_ref, grad_ref, basis_ref, out_ref, rows_ref):
    block = basis_ref.shape[0]
    step = pl.program_id(0)
    for i in range(block):
        masked_rows(ids_ref, step * block + i, basis_ref[i], rows_ref)
        out = jnp.dot(grad_ref[i], rows_ref[...], preferred_element_type=jnp.float32)
        out_ref[i] = out.astype(out_ref.dtype)


def pair_block(count):
    for size in (8, 4, 2, 1):
        if count % size == 0:
            return size


def synthesis(local_ids, spectral, lat_basis):
    pairs, width, length = spectral.shape
    half = lat_basis.shape[1]
    block = pair_block(pairs)
    spec = pltpu.PrefetchScalarGridSpec(
        num_scalar_prefetch=1,
        grid=(pairs // block,),
        in_specs=[
            pl.BlockSpec((block, width, length), lambda s, ids: (s, 0, 0)),
            pl.BlockSpec((block, half, length), lambda s, ids: (s, 0, 0)),
        ],
        out_specs=pl.BlockSpec((block, 4 * half, width), lambda s, ids: (s, 0, 0)),
        scratch_shapes=[pltpu.VMEM((4 * half, length), lat_basis.dtype)],
    )
    return pl.pallas_call(
        synth_kernel,
        grid_spec=spec,
        out_shape=jax.ShapeDtypeStruct((pairs, 4 * half, width), jnp.bfloat16),
    )(local_ids, spectral, lat_basis)


def analysis(local_ids, grads, lat_basis):
    pairs, width, rows = grads.shape
    half, length = lat_basis.shape[1], lat_basis.shape[2]
    block = pair_block(pairs)
    spec = pltpu.PrefetchScalarGridSpec(
        num_scalar_prefetch=1,
        grid=(pairs // block,),
        in_specs=[
            pl.BlockSpec((block, width, rows), lambda s, ids: (s, 0, 0)),
            pl.BlockSpec((block, half, length), lambda s, ids: (s, 0, 0)),
        ],
        out_specs=pl.BlockSpec((block, width, length), lambda s, ids: (s, 0, 0)),
        scratch_shapes=[pltpu.VMEM((4 * half, length), lat_basis.dtype)],
    )
    return pl.pallas_call(
        analyse_kernel,
        grid_spec=spec,
        out_shape=jax.ShapeDtypeStruct((pairs, width, length), jnp.bfloat16),
    )(local_ids, grads, lat_basis)


def per_device(
    pair_table, spectral, lat_basis, in_weight, in_bias, out_weight, out_bias, cotangent
):
    pair_dev = spectral.shape[0]
    width_local = spectral.shape[1]
    lat_half = lat_basis.shape[1]
    band_rows = cotangent.shape[0]
    block_cols = cotangent.shape[2]
    lon_total = block_cols * lax.axis_size("lon")
    first_row = lax.axis_index("lat") * pair_dev
    local_ids = lax.dynamic_slice_in_dim(pair_table, first_row, pair_dev)
    lat_window = 2 * lat_half
    raw_waves = synthesis(local_ids, spectral, lat_basis).reshape(
        pair_dev, 2, lat_window, width_local
    )
    waves = jnp.concatenate(
        [raw_waves[:, :, :lat_half], jnp.flip(raw_waves[:, :, lat_half:], axis=2)], axis=2
    )
    flat_waves = waves.reshape(2 * pair_dev, lat_window * width_local)
    band_waves = lax.all_to_all(flat_waves, "lat", split_axis=1, concat_axis=0, tiled=True)
    wave_count = band_waves.shape[0]
    coeff_grid = band_waves.reshape(wave_count, band_rows, width_local // 2, 2)
    numbers = wave_numbers(pair_table)
    full_table = fourier_table(numbers, lon_total)
    lon_parts = lax.axis_size("lon")
    block_table = full_table.reshape(2, wave_count, lon_parts, block_cols)
    all_columns = jnp.einsum(
        "glkc,cgbn->blkn", coeff_grid, block_table, preferred_element_type=jnp.float32
    ).astype(jnp.bfloat16)
    level_blocks = lax.all_to_all(all_columns, "lon", 0, 0, tiled=True)
    grid = jnp.swapaxes(level_blocks, 0, 1).reshape(band_rows, -1, block_cols)
    pre_act = (
        jnp.einsum("lkc,kh->lch", grid, in_weight, preferred_element_type=jnp.float32) + in_bias
    )
    activated, gelu_back = jax.vjp(jax.nn.gelu, pre_act)
    hidden = activated.astype(jnp.bfloat16)
    tendency = (
        jnp.einsum("lch,hk->lkc", hidden, out_weight, preferred_element_type=jnp.float32)
        + out_bias[None, :, None]
    ).astype(jnp.bfloat16)
    out_weight_part = jnp.einsum(
        "lch,lkc->kh", hidden, cotangent, preferred_element_type=jnp.float32
    )
    out_bias_part = jnp.sum(cotangent.astype(jnp.float32), axis=(0, 2))
    hidden_grad = jnp.einsum(
        "lkc,hk->lch", cotangent, out_weight, preferred_element_type=jnp.float32
    )
    pre_grad = gelu_back(hidden_grad)[0].astype(jnp.bfloat16)
    in_weight_part = jnp.einsum("lkc,lch->kh", grid, pre_grad, preferred_element_type=jnp.float32)
    in_bias_part = jnp.sum(pre_grad.astype(jnp.float32), axis=(0, 1))
    grid_grad = jnp.einsum(
        "lch,kh->lkc", pre_grad, in_weight, preferred_element_type=jnp.float32
    ).astype(jnp.bfloat16)
    channels, hid = in_weight.shape
    width = max(hid, channels)

    def widen(v):
        return jnp.pad(v, ((0, 0), (0, width - v.shape[1])))

    stacked = jnp.concatenate(
        [
            widen(in_weight_part),
            widen(out_weight_part),
            widen(in_bias_part[None, :]),
            widen(out_bias_part[None, :]),
        ],
        axis=0,
    )
    summed = all_reduce(stacked, ("lat", "lon"))
    in_weight_grad = summed[:channels, :hid]
    out_weight_grad = summed[channels : 2 * channels, :hid].T
    in_bias_grad = summed[2 * channels, :hid]
    out_bias_grad = summed[2 * channels + 1, :channels]
    grad_blocks = jnp.swapaxes(grid_grad.reshape(band_rows, lon_parts, -1, block_cols), 0, 1)
    level_rows = lax.all_to_all(grad_blocks, "lon", 0, 0, tiled=True)
    wave_grad = jnp.einsum(
        "cgbn,blkn->glkc", block_table, level_rows, preferred_element_type=jnp.float32
    ).astype(jnp.bfloat16)
    flat_grad = wave_grad.reshape(wave_count, band_rows * width_local)
    pair_grad = lax.all_to_all(flat_grad, "lat", split_axis=0, concat_axis=1, tiled=True)
    pair_grad = pair_grad.reshape(pair_dev, 2, lat_window, width_local)
    pair_grad = jnp.concatenate(
        [pair_grad[:, :, :lat_half], jnp.flip(pair_grad[:, :, lat_half:], axis=2)], axis=2
    )
    pair_grad = jnp.swapaxes(pair_grad.reshape(pair_dev, 2 * lat_window, width_local), 1, 2)
    spectral_grad = analysis(local_ids, pair_grad, lat_basis)
    return (tendency, spectral_grad, in_weight_grad, in_bias_grad, out_weight_grad, out_bias_grad)


def solution(mesh):
    placed = (
        P(),
        P("lat", "lon", None),
        P("lat", None, None),
        P(),
        P(),
        P(),
        P(),
        P("lat", None, "lon"),
    )
    return jax.shard_map(
        per_device,
        mesh=mesh,
        in_specs=placed,
        out_specs=(P("lat", None, "lon"), P("lat", "lon", None), P(), P(), P(), P()),
        check_vma=False,
    )
```

```python
import math

import jax
import jax.numpy as jnp
from jax import lax
from jax.experimental import pallas as pl
from jax.experimental.pallas import tpu as pltpu
from jax.sharding import PartitionSpec as P

TRUNC = 1279


def pair_masks(pair_ids, length):
    first_len = TRUNC + 1 - pair_ids
    position = jnp.arange(length, dtype=jnp.int32)[None, :]
    lower_part = position < first_len[:, None]
    upper_part = jnp.logical_and(position >= first_len[:, None], position < TRUNC + 2)
    offset = jnp.where(lower_part, position, position - first_len[:, None])
    parity = jnp.where(offset % 2 == 0, 1.0, -1.0).astype(jnp.float32)
    return (lower_part, upper_part, parity, first_len)


def wave_numbers(pair_ids):
    both = jnp.stack([pair_ids, TRUNC - pair_ids], axis=1)
    return both.reshape(-1)


def table_kernel(cos_a_ref, sin_a_ref, cos_b_ref, sin_b_ref, factor_ref, out_ref):
    fine = cos_b_ref.shape[1]
    cos_b = cos_b_ref[...]
    sin_b = sin_b_ref[...]
    factor = factor_ref[...]
    for u in range(cos_a_ref.shape[1]):
        cos_a = cos_a_ref[:, u : u + 1]
        sin_a = sin_a_ref[:, u : u + 1]
        cols = slice(u * fine, (u + 1) * fine)
        out_ref[0, :, cols] = (factor * (cos_a * cos_b - sin_a * sin_b)).astype(out_ref.dtype)
        out_ref[1, :, cols] = (-factor * (sin_a * cos_b + cos_a * sin_b)).astype(out_ref.dtype)


def fourier_table(numbers, lon_total):
    fine = 128
    count = numbers.shape[0]
    coarse = jnp.arange(lon_total // fine, dtype=jnp.int32) * fine
    scale = 2.0 * math.pi / lon_total

    def angles(offsets):
        phase = numbers[:, None] * offsets[None, :] % lon_total
        angle = phase.astype(jnp.float32) * scale
        return jnp.cos(angle), jnp.sin(angle)

    cos_a, sin_a = angles(coarse)
    cos_b, sin_b = angles(jnp.arange(fine, dtype=jnp.int32))
    factor = jnp.where(numbers == 0, 1.0, 2.0).astype(jnp.float32)[:, None]
    rows = 128 if count % 128 == 0 else count
    return pl.pallas_call(
        table_kernel,
        grid=(count // rows,),
        in_specs=[
            pl.BlockSpec((rows, coarse.shape[0]), lambda i: (i, 0)),
            pl.BlockSpec((rows, coarse.shape[0]), lambda i: (i, 0)),
            pl.BlockSpec((rows, fine), lambda i: (i, 0)),
            pl.BlockSpec((rows, fine), lambda i: (i, 0)),
            pl.BlockSpec((rows, 1), lambda i: (i, 0)),
        ],
        out_specs=pl.BlockSpec((2, rows, lon_total), lambda i: (0, i, 0)),
        out_shape=jax.ShapeDtypeStruct((2, count, lon_total), jnp.bfloat16),
    )(cos_a, sin_a, cos_b, sin_b, factor)


def all_reduce(value, axes):
    count = 1
    for name in axes:
        count *= lax.axis_size(name)
    flat = value.reshape(-1)
    chunk = -(-flat.shape[0] // (count * 128)) * 128
    flat = jnp.pad(flat, (0, chunk * count - flat.shape[0]))
    parts = lax.all_to_all(flat.reshape(count, chunk), axes, 0, 0, tiled=True)
    owned = jnp.sum(parts, axis=0, keepdims=True)
    spread = jnp.broadcast_to(owned, (count, chunk))
    whole = lax.all_to_all(spread, axes, 0, 0, tiled=True).reshape(-1)
    return whole[: value.size].reshape(value.shape)


def masked_rows(ids_ref, pair_index, basis, rows_ref):
    half, length = basis.shape
    pair = ids_ref[pair_index]
    first = TRUNC + 1 - pair
    position = lax.broadcasted_iota(jnp.int32, (1, length), 1)
    lower = position < first
    upper = jnp.logical_and(position >= first, position < TRUNC + 2)
    offset = jnp.where(lower, position, position - first)
    odd = offset % 2 == 1
    zero = jnp.zeros_like(basis)
    signed = jnp.where(odd, -basis, basis)
    rows_ref[0:half, :] = jnp.where(lower, basis, zero)
    rows_ref[half : 2 * half, :] = jnp.where(lower, signed, zero)
    rows_ref[2 * half : 3 * half, :] = jnp.where(upper, basis, zero)
    rows_ref[3 * half : 4 * half, :] = jnp.where(upper, signed, zero)


def synth_kernel(ids_ref, spec_ref, basis_ref, out_ref, rows_ref):
    block = basis_ref.shape[0]
    step = pl.program_id(0)
    for i in range(block):
        masked_rows(ids_ref, step * block + i, basis_ref[i], rows_ref)
        out = lax.dot_general(
            rows_ref[...], spec_ref[i], (((1,), (1,)), ((), ())),
            preferred_element_type=jnp.float32,
        )
        out_ref[i] = out.astype(out_ref.dtype)


def analyse_kernel(ids_ref, grad_ref, basis_ref, out_ref, rows_ref):
    block = basis_ref.shape[0]
    step = pl.program_id(0)
    for i in range(block):
        masked_rows(ids_ref, step * block + i, basis_ref[i], rows_ref)
        out = jnp.dot(grad_ref[i], rows_ref[...], preferred_element_type=jnp.float32)
        out_ref[i] = out.astype(out_ref.dtype)


def pair_block(count):
    for size in (16, 8, 4, 2, 1):
        if count % size == 0:
            return size


def synthesis(local_ids, spectral, lat_basis):
    pairs, width, length = spectral.shape
    half = lat_basis.shape[1]
    block = pair_block(pairs)
    spec = pltpu.PrefetchScalarGridSpec(
        num_scalar_prefetch=1,
        grid=(pairs // block,),
        in_specs=[
            pl.BlockSpec((block, width, length), lambda s, ids: (s, 0, 0)),
            pl.BlockSpec((block, half, length), lambda s, ids: (s, 0, 0)),
        ],
        out_specs=pl.BlockSpec((block, 4 * half, width), lambda s, ids: (s, 0, 0)),
        scratch_shapes=[pltpu.VMEM((4 * half, length), lat_basis.dtype)],
    )
    return pl.pallas_call(
        synth_kernel,
        grid_spec=spec,
        out_shape=jax.ShapeDtypeStruct((pairs, 4 * half, width), jnp.bfloat16),
    )(local_ids, spectral, lat_basis)


def analysis(local_ids, grads, lat_basis):
    pairs, width, rows = grads.shape
    half, length = lat_basis.shape[1], lat_basis.shape[2]
    block = pair_block(pairs)
    spec = pltpu.PrefetchScalarGridSpec(
        num_scalar_prefetch=1,
        grid=(pairs // block,),
        in_specs=[
            pl.BlockSpec((block, width, rows), lambda s, ids: (s, 0, 0)),
            pl.BlockSpec((block, half, length), lambda s, ids: (s, 0, 0)),
        ],
        out_specs=pl.BlockSpec((block, width, length), lambda s, ids: (s, 0, 0)),
        scratch_shapes=[pltpu.VMEM((4 * half, length), lat_basis.dtype)],
    )
    return pl.pallas_call(
        analyse_kernel,
        grid_spec=spec,
        out_shape=jax.ShapeDtypeStruct((pairs, width, length), jnp.bfloat16),
    )(local_ids, grads, lat_basis)


def per_device(
    pair_table, spectral, lat_basis, in_weight, in_bias, out_weight, out_bias, cotangent
):
    pair_dev = spectral.shape[0]
    width_local = spectral.shape[1]
    lat_half = lat_basis.shape[1]
    band_rows = cotangent.shape[0]
    block_cols = cotangent.shape[2]
    lon_total = block_cols * lax.axis_size("lon")
    first_row = lax.axis_index("lat") * pair_dev
    local_ids = lax.dynamic_slice_in_dim(pair_table, first_row, pair_dev)
    lat_window = 2 * lat_half
    raw_waves = synthesis(local_ids, spectral, lat_basis).reshape(
        pair_dev, 2, lat_window, width_local
    )
    lat_index = jnp.arange(lat_window, dtype=jnp.int32)
    kernel_row = jnp.where(lat_index < lat_half, lat_index, 3 * lat_half - 1 - lat_index)
    reorder = (kernel_row[:, None] == lat_index[None, :]).astype(jnp.bfloat16)
    waves = jnp.einsum(
        "lr,pqrk->pqlk", reorder, raw_waves, preferred_element_type=jnp.float32
    ).astype(jnp.bfloat16)
    flat_waves = waves.reshape(2 * pair_dev, lat_window * width_local)
    band_waves = lax.all_to_all(flat_waves, "lat", split_axis=1, concat_axis=0, tiled=True)
    wave_count = band_waves.shape[0]
    coeff_grid = band_waves.reshape(wave_count, band_rows, width_local // 2, 2)
    numbers = wave_numbers(pair_table)
    full_table = fourier_table(numbers, lon_total)
    lon_parts = lax.axis_size("lon")
    block_table = full_table.reshape(2, wave_count, lon_parts, block_cols)
    all_columns = jnp.einsum(
        "glkc,cgbn->blkn", coeff_grid, block_table, preferred_element_type=jnp.float32
    ).astype(jnp.bfloat16)
    level_blocks = lax.all_to_all(all_columns, "lon", 0, 0, tiled=True)
    grid = jnp.swapaxes(level_blocks, 0, 1).reshape(band_rows, -1, block_cols)
    pre_act = (
        jnp.einsum("lkc,kh->lch", grid, in_weight, preferred_element_type=jnp.float32) + in_bias
    )
    activated, gelu_back = jax.vjp(jax.nn.gelu, pre_act)
    hidden = activated.astype(jnp.bfloat16)
    tendency = (
        jnp.einsum("lch,hk->lkc", hidden, out_weight, preferred_element_type=jnp.float32)
        + out_bias[None, :, None]
    ).astype(jnp.bfloat16)
    out_weight_part = jnp.einsum(
        "lch,lkc->kh", hidden, cotangent, preferred_element_type=jnp.float32
    )
    out_bias_part = jnp.sum(cotangent.astype(jnp.float32), axis=(0, 2))
    hidden_grad = jnp.einsum(
        "lkc,hk->lch", cotangent, out_weight, preferred_element_type=jnp.float32
    )
    pre_grad = gelu_back(hidden_grad)[0].astype(jnp.bfloat16)
    in_weight_part = jnp.einsum("lkc,lch->kh", grid, pre_grad, preferred_element_type=jnp.float32)
    in_bias_part = jnp.sum(pre_grad.astype(jnp.float32), axis=(0, 1))
    grid_grad = jnp.einsum(
        "lch,kh->lkc", pre_grad, in_weight, preferred_element_type=jnp.float32
    ).astype(jnp.bfloat16)
    channels, hid = in_weight.shape
    width = max(hid, channels)

    def widen(v):
        return jnp.pad(v, ((0, 0), (0, width - v.shape[1])))

    stacked = jnp.concatenate(
        [
            widen(in_weight_part),
            widen(out_weight_part),
            widen(in_bias_part[None, :]),
            widen(out_bias_part[None, :]),
        ],
        axis=0,
    )
    summed = all_reduce(stacked, ("lat", "lon"))
    in_weight_grad = summed[:channels, :hid]
    out_weight_grad = summed[channels : 2 * channels, :hid].T
    in_bias_grad = summed[2 * channels, :hid]
    out_bias_grad = summed[2 * channels + 1, :channels]
    grad_blocks = jnp.swapaxes(grid_grad.reshape(band_rows, lon_parts, -1, block_cols), 0, 1)
    level_rows = lax.all_to_all(grad_blocks, "lon", 0, 0, tiled=True)
    wave_grad = jnp.einsum(
        "cgbn,blkn->glkc", block_table, level_rows, preferred_element_type=jnp.float32
    ).astype(jnp.bfloat16)
    flat_grad = wave_grad.reshape(wave_count, band_rows * width_local)
    pair_grad = lax.all_to_all(flat_grad, "lat", split_axis=0, concat_axis=1, tiled=True)
    pair_grad = pair_grad.reshape(pair_dev, 2, lat_window, width_local)
    pair_grad = jnp.einsum(
        "lr,pqlk->pkqr", reorder, pair_grad, preferred_element_type=jnp.float32
    ).astype(jnp.bfloat16).reshape(pair_dev, width_local, 2 * lat_window)
    spectral_grad = analysis(local_ids, pair_grad, lat_basis)
    return (tendency, spectral_grad, in_weight_grad, in_bias_grad, out_weight_grad, out_bias_grad)


def solution(mesh):
    placed = (
        P(),
        P("lat", "lon", None),
        P("lat", None, None),
        P(),
        P(),
        P(),
        P(),
        P("lat", None, "lon"),
    )
    return jax.shard_map(
        per_device,
        mesh=mesh,
        in_specs=placed,
        out_specs=(P("lat", None, "lon"), P("lat", "lon", None), P(), P(), P(), P()),
        check_vma=False,
    )
```

```python
import math

import jax
import jax.numpy as jnp
from jax import lax
from jax.experimental import pallas as pl
from jax.experimental.pallas import tpu as pltpu
from jax.sharding import PartitionSpec as P

TRUNC = 1279


def pair_masks(pair_ids, length):
    first_len = TRUNC + 1 - pair_ids
    position = jnp.arange(length, dtype=jnp.int32)[None, :]
    lower_part = position < first_len[:, None]
    upper_part = jnp.logical_and(position >= first_len[:, None], position < TRUNC + 2)
    offset = jnp.where(lower_part, position, position - first_len[:, None])
    parity = jnp.where(offset % 2 == 0, 1.0, -1.0).astype(jnp.float32)
    return (lower_part, upper_part, parity, first_len)


def wave_numbers(pair_ids):
    both = jnp.stack([pair_ids, TRUNC - pair_ids], axis=1)
    return both.reshape(-1)


def table_kernel(cos_a_ref, sin_a_ref, cos_b_ref, sin_b_ref, factor_ref, out_ref):
    fine = cos_b_ref.shape[1]
    cos_b = cos_b_ref[...]
    sin_b = sin_b_ref[...]
    factor = factor_ref[...]
    for u in range(cos_a_ref.shape[1]):
        cos_a = cos_a_ref[:, u : u + 1]
        sin_a = sin_a_ref[:, u : u + 1]
        cols = slice(u * fine, (u + 1) * fine)
        out_ref[0, :, cols] = (factor * (cos_a * cos_b - sin_a * sin_b)).astype(out_ref.dtype)
        out_ref[1, :, cols] = (-factor * (sin_a * cos_b + cos_a * sin_b)).astype(out_ref.dtype)


def fourier_table(numbers, lon_total):
    fine = 128
    count = numbers.shape[0]
    coarse = jnp.arange(lon_total // fine, dtype=jnp.int32) * fine
    scale = 2.0 * math.pi / lon_total

    def angles(offsets):
        phase = numbers[:, None] * offsets[None, :] % lon_total
        angle = phase.astype(jnp.float32) * scale
        return jnp.cos(angle), jnp.sin(angle)

    cos_a, sin_a = angles(coarse)
    cos_b, sin_b = angles(jnp.arange(fine, dtype=jnp.int32))
    factor = jnp.where(numbers == 0, 1.0, 2.0).astype(jnp.float32)[:, None]
    rows = 128 if count % 128 == 0 else count
    return pl.pallas_call(
        table_kernel,
        grid=(count // rows,),
        in_specs=[
            pl.BlockSpec((rows, coarse.shape[0]), lambda i: (i, 0)),
            pl.BlockSpec((rows, coarse.shape[0]), lambda i: (i, 0)),
            pl.BlockSpec((rows, fine), lambda i: (i, 0)),
            pl.BlockSpec((rows, fine), lambda i: (i, 0)),
            pl.BlockSpec((rows, 1), lambda i: (i, 0)),
        ],
        out_specs=pl.BlockSpec((2, rows, lon_total), lambda i: (0, i, 0)),
        out_shape=jax.ShapeDtypeStruct((2, count, lon_total), jnp.bfloat16),
    )(cos_a, sin_a, cos_b, sin_b, factor)


def all_reduce(value, axes):
    count = 1
    for name in axes:
        count *= lax.axis_size(name)
    flat = value.reshape(-1)
    chunk = -(-flat.shape[0] // (count * 128)) * 128
    flat = jnp.pad(flat, (0, chunk * count - flat.shape[0]))
    sent = flat.reshape(count, chunk).astype(jnp.bfloat16)
    parts = lax.all_to_all(sent, axes, 0, 0, tiled=True)
    owned = jnp.sum(parts.astype(jnp.float32), axis=0, keepdims=True)
    spread = jnp.broadcast_to(owned, (count, chunk))
    whole = lax.all_to_all(spread, axes, 0, 0, tiled=True).reshape(-1)
    return whole[: value.size].reshape(value.shape)


def masked_rows(ids_ref, pair_index, basis, rows_ref):
    half, length = basis.shape
    pair = ids_ref[pair_index]
    first = TRUNC + 1 - pair
    position = lax.broadcasted_iota(jnp.int32, (1, length), 1)
    lower = position < first
    upper = jnp.logical_and(position >= first, position < TRUNC + 2)
    offset = jnp.where(lower, position, position - first)
    odd = offset % 2 == 1
    zero = jnp.zeros_like(basis)
    signed = jnp.where(odd, -basis, basis)
    rows_ref[0:half, :] = jnp.where(lower, basis, zero)
    rows_ref[half : 2 * half, :] = jnp.where(lower, signed, zero)
    rows_ref[2 * half : 3 * half, :] = jnp.where(upper, basis, zero)
    rows_ref[3 * half : 4 * half, :] = jnp.where(upper, signed, zero)


def synth_kernel(ids_ref, spec_ref, basis_ref, out_ref, rows_ref):
    block = basis_ref.shape[0]
    step = pl.program_id(0)
    for i in range(block):
        masked_rows(ids_ref, step * block + i, basis_ref[i], rows_ref)
        out = lax.dot_general(
            rows_ref[...], spec_ref[i], (((1,), (1,)), ((), ())),
            preferred_element_type=jnp.float32,
        )
        out_ref[i] = out.astype(out_ref.dtype)


def analyse_kernel(ids_ref, grad_ref, basis_ref, out_ref, rows_ref):
    block = basis_ref.shape[0]
    step = pl.program_id(0)
    for i in range(block):
        masked_rows(ids_ref, step * block + i, basis_ref[i], rows_ref)
        out = jnp.dot(grad_ref[i], rows_ref[...], preferred_element_type=jnp.float32)
        out_ref[i] = out.astype(out_ref.dtype)


def pair_block(count):
    for size in (16, 8, 4, 2, 1):
        if count % size == 0:
            return size


def synthesis(local_ids, spectral, lat_basis):
    pairs, width, length = spectral.shape
    half = lat_basis.shape[1]
    block = pair_block(pairs)
    spec = pltpu.PrefetchScalarGridSpec(
        num_scalar_prefetch=1,
        grid=(pairs // block,),
        in_specs=[
            pl.BlockSpec((block, width, length), lambda s, ids: (s, 0, 0)),
            pl.BlockSpec((block, half, length), lambda s, ids: (s, 0, 0)),
        ],
        out_specs=pl.BlockSpec((block, 4 * half, width), lambda s, ids: (s, 0, 0)),
        scratch_shapes=[pltpu.VMEM((4 * half, length), lat_basis.dtype)],
    )
    return pl.pallas_call(
        synth_kernel,
        grid_spec=spec,
        out_shape=jax.ShapeDtypeStruct((pairs, 4 * half, width), jnp.bfloat16),
    )(local_ids, spectral, lat_basis)


def analysis(local_ids, grads, lat_basis):
    pairs, width, rows = grads.shape
    half, length = lat_basis.shape[1], lat_basis.shape[2]
    block = pair_block(pairs)
    spec = pltpu.PrefetchScalarGridSpec(
        num_scalar_prefetch=1,
        grid=(pairs // block,),
        in_specs=[
            pl.BlockSpec((block, width, rows), lambda s, ids: (s, 0, 0)),
            pl.BlockSpec((block, half, length), lambda s, ids: (s, 0, 0)),
        ],
        out_specs=pl.BlockSpec((block, width, length), lambda s, ids: (s, 0, 0)),
        scratch_shapes=[pltpu.VMEM((4 * half, length), lat_basis.dtype)],
    )
    return pl.pallas_call(
        analyse_kernel,
        grid_spec=spec,
        out_shape=jax.ShapeDtypeStruct((pairs, width, length), jnp.bfloat16),
    )(local_ids, grads, lat_basis)


def per_device(
    pair_table, spectral, lat_basis, in_weight, in_bias, out_weight, out_bias, cotangent
):
    pair_dev = spectral.shape[0]
    width_local = spectral.shape[1]
    lat_half = lat_basis.shape[1]
    band_rows = cotangent.shape[0]
    block_cols = cotangent.shape[2]
    lon_total = block_cols * lax.axis_size("lon")
    first_row = lax.axis_index("lat") * pair_dev
    local_ids = lax.dynamic_slice_in_dim(pair_table, first_row, pair_dev)
    lat_window = 2 * lat_half
    raw_waves = synthesis(local_ids, spectral, lat_basis).reshape(
        pair_dev, 2, lat_window, width_local
    )
    lat_index = jnp.arange(lat_window, dtype=jnp.int32)
    kernel_row = jnp.where(lat_index < lat_half, lat_index, 3 * lat_half - 1 - lat_index)
    reorder = (kernel_row[:, None] == lat_index[None, :]).astype(jnp.bfloat16)
    waves = jnp.einsum(
        "lr,pqrk->pqlk", reorder, raw_waves, preferred_element_type=jnp.float32
    ).astype(jnp.bfloat16)
    flat_waves = waves.reshape(2 * pair_dev, lat_window * width_local)
    band_waves = lax.all_to_all(flat_waves, "lat", split_axis=1, concat_axis=0, tiled=True)
    wave_count = band_waves.shape[0]
    coeff_grid = band_waves.reshape(wave_count, band_rows, width_local // 2, 2)
    numbers = wave_numbers(pair_table)
    full_table = fourier_table(numbers, lon_total)
    lon_parts = lax.axis_size("lon")
    block_table = full_table.reshape(2, wave_count, lon_parts, block_cols)
    all_columns = jnp.einsum(
        "glkc,cgbn->blkn", coeff_grid, block_table, preferred_element_type=jnp.float32
    ).astype(jnp.bfloat16)
    level_blocks = lax.all_to_all(all_columns, "lon", 0, 0, tiled=True)
    grid = jnp.swapaxes(level_blocks, 0, 1).reshape(band_rows, -1, block_cols)
    pre_act = (
        jnp.einsum("lkc,kh->lch", grid, in_weight, preferred_element_type=jnp.float32) + in_bias
    )
    activated, gelu_back = jax.vjp(jax.nn.gelu, pre_act)
    hidden = activated.astype(jnp.bfloat16)
    tendency = (
        jnp.einsum("lch,hk->lkc", hidden, out_weight, preferred_element_type=jnp.float32)
        + out_bias[None, :, None]
    ).astype(jnp.bfloat16)
    out_weight_part = jnp.einsum(
        "lch,lkc->kh", hidden, cotangent, preferred_element_type=jnp.float32
    )
    out_bias_part = jnp.sum(cotangent.astype(jnp.float32), axis=(0, 2))
    hidden_grad = jnp.einsum(
        "lkc,hk->lch", cotangent, out_weight, preferred_element_type=jnp.float32
    )
    pre_grad = gelu_back(hidden_grad)[0].astype(jnp.bfloat16)
    in_weight_part = jnp.einsum("lkc,lch->kh", grid, pre_grad, preferred_element_type=jnp.float32)
    in_bias_part = jnp.sum(pre_grad.astype(jnp.float32), axis=(0, 1))
    grid_grad = jnp.einsum(
        "lch,kh->lkc", pre_grad, in_weight, preferred_element_type=jnp.float32
    ).astype(jnp.bfloat16)
    channels, hid = in_weight.shape
    width = max(hid, channels)

    def widen(v):
        return jnp.pad(v, ((0, 0), (0, width - v.shape[1])))

    stacked = jnp.concatenate(
        [
            widen(in_weight_part),
            widen(out_weight_part),
            widen(in_bias_part[None, :]),
            widen(out_bias_part[None, :]),
        ],
        axis=0,
    )
    summed = all_reduce(stacked, ("lat", "lon"))
    in_weight_grad = summed[:channels, :hid]
    out_weight_grad = summed[channels : 2 * channels, :hid].T
    in_bias_grad = summed[2 * channels, :hid]
    out_bias_grad = summed[2 * channels + 1, :channels]
    grad_blocks = jnp.swapaxes(grid_grad.reshape(band_rows, lon_parts, -1, block_cols), 0, 1)
    level_rows = lax.all_to_all(grad_blocks, "lon", 0, 0, tiled=True)
    wave_grad = jnp.einsum(
        "cgbn,blkn->glkc", block_table, level_rows, preferred_element_type=jnp.float32
    ).astype(jnp.bfloat16)
    flat_grad = wave_grad.reshape(wave_count, band_rows * width_local)
    pair_grad = lax.all_to_all(flat_grad, "lat", split_axis=0, concat_axis=1, tiled=True)
    pair_grad = pair_grad.reshape(pair_dev, 2, lat_window, width_local)
    pair_grad = jnp.einsum(
        "lr,pqlk->pkqr", reorder, pair_grad, preferred_element_type=jnp.float32
    ).astype(jnp.bfloat16).reshape(pair_dev, width_local, 2 * lat_window)
    spectral_grad = analysis(local_ids, pair_grad, lat_basis)
    return (tendency, spectral_grad, in_weight_grad, in_bias_grad, out_weight_grad, out_bias_grad)


def solution(mesh):
    placed = (
        P(),
        P("lat", "lon", None),
        P("lat", None, None),
        P(),
        P(),
        P(),
        P(),
        P("lat", None, "lon"),
    )
    return jax.shard_map(
        per_device,
        mesh=mesh,
        in_specs=placed,
        out_specs=(P("lat", None, "lon"), P("lat", "lon", None), P(), P(), P(), P()),
        check_vma=False,
    )
```

```python
import math

import jax
import jax.numpy as jnp
from jax import lax
from jax.experimental import pallas as pl
from jax.experimental.pallas import tpu as pltpu
from jax.sharding import PartitionSpec as P

TRUNC = 1279


def pair_masks(pair_ids, length):
    first_len = TRUNC + 1 - pair_ids
    position = jnp.arange(length, dtype=jnp.int32)[None, :]
    lower_part = position < first_len[:, None]
    upper_part = jnp.logical_and(position >= first_len[:, None], position < TRUNC + 2)
    offset = jnp.where(lower_part, position, position - first_len[:, None])
    parity = jnp.where(offset % 2 == 0, 1.0, -1.0).astype(jnp.float32)
    return (lower_part, upper_part, parity, first_len)


def wave_numbers(pair_ids):
    both = jnp.stack([pair_ids, TRUNC - pair_ids], axis=1)
    return both.reshape(-1)


def table_kernel(cos_a_ref, sin_a_ref, cos_b_ref, sin_b_ref, factor_ref, out_ref):
    fine = cos_b_ref.shape[1]
    cos_b = cos_b_ref[...]
    sin_b = sin_b_ref[...]
    factor = factor_ref[...]
    for u in range(cos_a_ref.shape[1]):
        cos_a = cos_a_ref[:, u : u + 1]
        sin_a = sin_a_ref[:, u : u + 1]
        cols = slice(u * fine, (u + 1) * fine)
        out_ref[0, :, cols] = (factor * (cos_a * cos_b - sin_a * sin_b)).astype(out_ref.dtype)
        out_ref[1, :, cols] = (-factor * (sin_a * cos_b + cos_a * sin_b)).astype(out_ref.dtype)


def fourier_table(numbers, lon_total):
    fine = 128
    count = numbers.shape[0]
    coarse = jnp.arange(lon_total // fine, dtype=jnp.int32) * fine
    scale = 2.0 * math.pi / lon_total

    def angles(offsets):
        phase = numbers[:, None] * offsets[None, :] % lon_total
        angle = phase.astype(jnp.float32) * scale
        return jnp.cos(angle), jnp.sin(angle)

    cos_a, sin_a = angles(coarse)
    cos_b, sin_b = angles(jnp.arange(fine, dtype=jnp.int32))
    factor = jnp.where(numbers == 0, 1.0, 2.0).astype(jnp.float32)[:, None]
    rows = 128 if count % 128 == 0 else count
    return pl.pallas_call(
        table_kernel,
        grid=(count // rows,),
        in_specs=[
            pl.BlockSpec((rows, coarse.shape[0]), lambda i: (i, 0)),
            pl.BlockSpec((rows, coarse.shape[0]), lambda i: (i, 0)),
            pl.BlockSpec((rows, fine), lambda i: (i, 0)),
            pl.BlockSpec((rows, fine), lambda i: (i, 0)),
            pl.BlockSpec((rows, 1), lambda i: (i, 0)),
        ],
        out_specs=pl.BlockSpec((2, rows, lon_total), lambda i: (0, i, 0)),
        out_shape=jax.ShapeDtypeStruct((2, count, lon_total), jnp.bfloat16),
    )(cos_a, sin_a, cos_b, sin_b, factor)


def all_reduce(value, axes):
    count = 1
    for name in axes:
        count *= lax.axis_size(name)
    flat = value.reshape(-1)
    chunk = -(-flat.shape[0] // (count * 128)) * 128
    flat = jnp.pad(flat, (0, chunk * count - flat.shape[0]))
    sent = flat.reshape(count, chunk).astype(jnp.bfloat16)
    parts = lax.all_to_all(sent, axes, 0, 0, tiled=True)
    owned = jnp.sum(parts.astype(jnp.float32), axis=0, keepdims=True)
    spread = jnp.broadcast_to(owned, (count, chunk))
    whole = lax.all_to_all(spread, axes, 0, 0, tiled=True).reshape(-1)
    return whole[: value.size].reshape(value.shape)


def masked_rows(ids_ref, pair_index, basis, rows_ref):
    half, length = basis.shape
    pair = ids_ref[pair_index]
    first = TRUNC + 1 - pair
    position = lax.broadcasted_iota(jnp.int32, (1, length), 1)
    lower = position < first
    upper = jnp.logical_and(position >= first, position < TRUNC + 2)
    offset = jnp.where(lower, position, position - first)
    odd = offset % 2 == 1
    zero = jnp.zeros_like(basis)
    signed = jnp.where(odd, -basis, basis)
    rows_ref[0:half, :] = jnp.where(lower, basis, zero)
    rows_ref[half : 2 * half, :] = jnp.where(lower, signed, zero)
    rows_ref[2 * half : 3 * half, :] = jnp.where(upper, basis, zero)
    rows_ref[3 * half : 4 * half, :] = jnp.where(upper, signed, zero)


def synth_kernel(ids_ref, spec_ref, basis_ref, out_ref, rows_ref):
    block = basis_ref.shape[0]
    step = pl.program_id(0)
    for i in range(block):
        masked_rows(ids_ref, step * block + i, basis_ref[i], rows_ref)
        out = lax.dot_general(
            rows_ref[...], spec_ref[i], (((1,), (1,)), ((), ())),
            preferred_element_type=jnp.float32,
        )
        out_ref[i] = out.astype(out_ref.dtype)


def analyse_kernel(ids_ref, grad_ref, basis_ref, out_ref, rows_ref):
    block = basis_ref.shape[0]
    step = pl.program_id(0)
    for i in range(block):
        masked_rows(ids_ref, step * block + i, basis_ref[i], rows_ref)
        out = jnp.dot(grad_ref[i], rows_ref[...], preferred_element_type=jnp.float32)
        out_ref[i] = out.astype(out_ref.dtype)


def pair_block(count):
    for size in (16, 8, 4, 2, 1):
        if count % size == 0:
            return size


def synthesis(local_ids, spectral, lat_basis):
    pairs, width, length = spectral.shape
    half = lat_basis.shape[1]
    block = pair_block(pairs)
    spec = pltpu.PrefetchScalarGridSpec(
        num_scalar_prefetch=1,
        grid=(pairs // block,),
        in_specs=[
            pl.BlockSpec((block, width, length), lambda s, ids: (s, 0, 0)),
            pl.BlockSpec((block, half, length), lambda s, ids: (s, 0, 0)),
        ],
        out_specs=pl.BlockSpec((block, 4 * half, width), lambda s, ids: (s, 0, 0)),
        scratch_shapes=[pltpu.VMEM((4 * half, length), lat_basis.dtype)],
    )
    return pl.pallas_call(
        synth_kernel,
        grid_spec=spec,
        out_shape=jax.ShapeDtypeStruct((pairs, 4 * half, width), jnp.bfloat16),
    )(local_ids, spectral, lat_basis)


def analysis(local_ids, grads, lat_basis):
    pairs, width, rows = grads.shape
    half, length = lat_basis.shape[1], lat_basis.shape[2]
    block = pair_block(pairs)
    spec = pltpu.PrefetchScalarGridSpec(
        num_scalar_prefetch=1,
        grid=(pairs // block,),
        in_specs=[
            pl.BlockSpec((block, width, rows), lambda s, ids: (s, 0, 0)),
            pl.BlockSpec((block, half, length), lambda s, ids: (s, 0, 0)),
        ],
        out_specs=pl.BlockSpec((block, width, length), lambda s, ids: (s, 0, 0)),
        scratch_shapes=[pltpu.VMEM((4 * half, length), lat_basis.dtype)],
    )
    return pl.pallas_call(
        analyse_kernel,
        grid_spec=spec,
        out_shape=jax.ShapeDtypeStruct((pairs, width, length), jnp.bfloat16),
    )(local_ids, grads, lat_basis)


def fourier_kernel(wave_ref, table_ref, out_ref, acc_ref):
    source = pl.program_id(1)

    @pl.when(source == 0)
    def _():
        acc_ref[...] = jnp.zeros_like(acc_ref)

    table = table_ref[...]
    table = table.reshape(table.shape[0] * table.shape[1], table.shape[2])
    acc_ref[...] += jnp.dot(wave_ref[0], table, preferred_element_type=jnp.float32)

    @pl.when(source == pl.num_programs(1) - 1)
    def _():
        out_ref[0] = acc_ref[...].astype(out_ref.dtype)


def fourier_synthesis(waves, table, lon_parts):
    sources, rows, width = waves.shape
    per_source = width // 2
    lon_total = table.shape[2]
    block = lon_total // lon_parts
    return pl.pallas_call(
        fourier_kernel,
        grid=(lon_parts, sources),
        in_specs=[
            pl.BlockSpec((1, rows, width), lambda b, s: (s, 0, 0)),
            pl.BlockSpec((2, per_source, block), lambda b, s: (0, s, b)),
        ],
        out_specs=pl.BlockSpec((1, rows, block), lambda b, s: (b, 0, 0)),
        out_shape=jax.ShapeDtypeStruct((lon_parts, rows, block), jnp.bfloat16),
        scratch_shapes=[pltpu.VMEM((rows, block), jnp.float32)],
    )(waves, table)


def per_device(
    pair_table, spectral, lat_basis, in_weight, in_bias, out_weight, out_bias, cotangent
):
    pair_dev = spectral.shape[0]
    width_local = spectral.shape[1]
    lat_half = lat_basis.shape[1]
    band_rows = cotangent.shape[0]
    block_cols = cotangent.shape[2]
    lon_total = block_cols * lax.axis_size("lon")
    first_row = lax.axis_index("lat") * pair_dev
    local_ids = lax.dynamic_slice_in_dim(pair_table, first_row, pair_dev)
    lat_window = 2 * lat_half
    raw_waves = synthesis(local_ids, spectral, lat_basis).reshape(
        pair_dev, 2, lat_window, width_local
    )
    lat_index = jnp.arange(lat_window, dtype=jnp.int32)
    kernel_row = jnp.where(lat_index < lat_half, lat_index, 3 * lat_half - 1 - lat_index)
    reorder = (kernel_row[:, None] == lat_index[None, :]).astype(jnp.bfloat16)
    lat_parts = lax.axis_size("lat")
    lon_parts = lax.axis_size("lon")
    channels_local = width_local // 2
    waves = jnp.einsum(
        "lr,pqrkc->lkcpq",
        reorder,
        raw_waves.reshape(pair_dev, 2, lat_window, channels_local, 2),
        preferred_element_type=jnp.float32,
    ).astype(jnp.bfloat16)
    waves = waves.reshape(lat_parts, band_rows * channels_local, 2 * 2 * pair_dev)
    band_waves = lax.all_to_all(waves, "lat", 0, 0, tiled=True)
    wave_count = 2 * pair_dev * lat_parts
    numbers = wave_numbers(pair_table)
    full_table = fourier_table(numbers, lon_total)
    block_table = full_table.reshape(2, wave_count, lon_parts, block_cols)
    per_source = 2 * pair_dev
    if block_cols % 128 == 0 and per_source % 16 == 0:
        all_columns = fourier_synthesis(band_waves, full_table, lon_parts)
    else:
        all_columns = jnp.einsum(
            "srcw,cswbn->brn",
            band_waves.reshape(lat_parts, -1, 2, per_source),
            full_table.reshape(2, lat_parts, per_source, lon_parts, block_cols),
            preferred_element_type=jnp.float32,
        ).astype(jnp.bfloat16)
    all_columns = all_columns.reshape(lon_parts, band_rows, channels_local, block_cols)
    level_blocks = lax.all_to_all(all_columns, "lon", 0, 0, tiled=True)
    grid = jnp.swapaxes(level_blocks, 0, 1).reshape(band_rows, -1, block_cols)
    pre_act = (
        jnp.einsum("lkc,kh->lch", grid, in_weight, preferred_element_type=jnp.float32) + in_bias
    )
    activated, gelu_back = jax.vjp(jax.nn.gelu, pre_act)
    hidden = activated.astype(jnp.bfloat16)
    tendency = (
        jnp.einsum("lch,hk->lkc", hidden, out_weight, preferred_element_type=jnp.float32)
        + out_bias[None, :, None]
    ).astype(jnp.bfloat16)
    out_weight_part = jnp.einsum(
        "lch,lkc->kh", hidden, cotangent, preferred_element_type=jnp.float32
    )
    out_bias_part = jnp.sum(cotangent.astype(jnp.float32), axis=(0, 2))
    hidden_grad = jnp.einsum(
        "lkc,hk->lch", cotangent, out_weight, preferred_element_type=jnp.float32
    )
    pre_grad = gelu_back(hidden_grad)[0].astype(jnp.bfloat16)
    in_weight_part = jnp.einsum("lkc,lch->kh", grid, pre_grad, preferred_element_type=jnp.float32)
    in_bias_part = jnp.sum(pre_grad.astype(jnp.float32), axis=(0, 1))
    grid_grad = jnp.einsum(
        "lch,kh->lkc", pre_grad, in_weight, preferred_element_type=jnp.float32
    ).astype(jnp.bfloat16)
    channels, hid = in_weight.shape
    width = max(hid, channels)

    def widen(v):
        return jnp.pad(v, ((0, 0), (0, width - v.shape[1])))

    stacked = jnp.concatenate(
        [
            widen(in_weight_part),
            widen(out_weight_part),
            widen(in_bias_part[None, :]),
            widen(out_bias_part[None, :]),
        ],
        axis=0,
    )
    summed = all_reduce(stacked, ("lat", "lon"))
    in_weight_grad = summed[:channels, :hid]
    out_weight_grad = summed[channels : 2 * channels, :hid].T
    in_bias_grad = summed[2 * channels, :hid]
    out_bias_grad = summed[2 * channels + 1, :channels]
    grad_blocks = jnp.swapaxes(grid_grad.reshape(band_rows, lon_parts, -1, block_cols), 0, 1)
    level_rows = lax.all_to_all(grad_blocks, "lon", 0, 0, tiled=True)
    wave_grad = jnp.einsum(
        "cgbn,blkn->glkc", block_table, level_rows, preferred_element_type=jnp.float32
    ).astype(jnp.bfloat16)
    flat_grad = wave_grad.reshape(wave_count, band_rows * width_local)
    pair_grad = lax.all_to_all(flat_grad, "lat", split_axis=0, concat_axis=1, tiled=True)
    pair_grad = pair_grad.reshape(pair_dev, 2, lat_window, width_local)
    pair_grad = jnp.einsum(
        "lr,pqlk->pkqr", reorder, pair_grad, preferred_element_type=jnp.float32
    ).astype(jnp.bfloat16).reshape(pair_dev, width_local, 2 * lat_window)
    spectral_grad = analysis(local_ids, pair_grad, lat_basis)
    return (tendency, spectral_grad, in_weight_grad, in_bias_grad, out_weight_grad, out_bias_grad)


def solution(mesh):
    placed = (
        P(),
        P("lat", "lon", None),
        P("lat", None, None),
        P(),
        P(),
        P(),
        P(),
        P("lat", None, "lon"),
    )
    return jax.shard_map(
        per_device,
        mesh=mesh,
        in_specs=placed,
        out_specs=(P("lat", None, "lon"), P("lat", "lon", None), P(), P(), P(), P()),
        check_vma=False,
    )
```

```python
import math

import jax
import jax.numpy as jnp
from jax import lax
from jax.experimental import pallas as pl
from jax.experimental.pallas import tpu as pltpu
from jax.sharding import PartitionSpec as P

TRUNC = 1279


def pair_masks(pair_ids, length):
    first_len = TRUNC + 1 - pair_ids
    position = jnp.arange(length, dtype=jnp.int32)[None, :]
    lower_part = position < first_len[:, None]
    upper_part = jnp.logical_and(position >= first_len[:, None], position < TRUNC + 2)
    offset = jnp.where(lower_part, position, position - first_len[:, None])
    parity = jnp.where(offset % 2 == 0, 1.0, -1.0).astype(jnp.float32)
    return (lower_part, upper_part, parity, first_len)


def wave_numbers(pair_ids):
    both = jnp.stack([pair_ids, TRUNC - pair_ids], axis=1)
    return both.reshape(-1)


def table_kernel(cos_a_ref, sin_a_ref, cos_b_ref, sin_b_ref, factor_ref, out_ref):
    fine = cos_b_ref.shape[1]
    cos_b = cos_b_ref[...]
    sin_b = sin_b_ref[...]
    factor = factor_ref[...]
    for u in range(cos_a_ref.shape[1]):
        cos_a = cos_a_ref[:, u : u + 1]
        sin_a = sin_a_ref[:, u : u + 1]
        cols = slice(u * fine, (u + 1) * fine)
        out_ref[0, :, cols] = (factor * (cos_a * cos_b - sin_a * sin_b)).astype(out_ref.dtype)
        out_ref[1, :, cols] = (-factor * (sin_a * cos_b + cos_a * sin_b)).astype(out_ref.dtype)


def fourier_table(numbers, lon_total):
    fine = 128
    count = numbers.shape[0]
    coarse = jnp.arange(lon_total // fine, dtype=jnp.int32) * fine
    scale = 2.0 * math.pi / lon_total

    def angles(offsets):
        phase = numbers[:, None] * offsets[None, :] % lon_total
        angle = phase.astype(jnp.float32) * scale
        return jnp.cos(angle), jnp.sin(angle)

    cos_a, sin_a = angles(coarse)
    cos_b, sin_b = angles(jnp.arange(fine, dtype=jnp.int32))
    factor = jnp.where(numbers == 0, 1.0, 2.0).astype(jnp.float32)[:, None]
    rows = 128 if count % 128 == 0 else count
    return pl.pallas_call(
        table_kernel,
        grid=(count // rows,),
        in_specs=[
            pl.BlockSpec((rows, coarse.shape[0]), lambda i: (i, 0)),
            pl.BlockSpec((rows, coarse.shape[0]), lambda i: (i, 0)),
            pl.BlockSpec((rows, fine), lambda i: (i, 0)),
            pl.BlockSpec((rows, fine), lambda i: (i, 0)),
            pl.BlockSpec((rows, 1), lambda i: (i, 0)),
        ],
        out_specs=pl.BlockSpec((2, rows, lon_total), lambda i: (0, i, 0)),
        out_shape=jax.ShapeDtypeStruct((2, count, lon_total), jnp.bfloat16),
    )(cos_a, sin_a, cos_b, sin_b, factor)


def all_reduce(value, axes):
    count = 1
    for name in axes:
        count *= lax.axis_size(name)
    flat = value.reshape(-1)
    chunk = -(-flat.shape[0] // (count * 128)) * 128
    flat = jnp.pad(flat, (0, chunk * count - flat.shape[0]))
    sent = flat.reshape(count, chunk).astype(jnp.bfloat16)
    parts = lax.all_to_all(sent, axes, 0, 0, tiled=True)
    owned = jnp.sum(parts.astype(jnp.float32), axis=0, keepdims=True)
    spread = jnp.broadcast_to(owned, (count, chunk))
    whole = lax.all_to_all(spread, axes, 0, 0, tiled=True).reshape(-1)
    return whole[: value.size].reshape(value.shape)


def masked_rows(ids_ref, pair_index, basis, rows_ref):
    half, length = basis.shape
    pair = ids_ref[pair_index]
    first = TRUNC + 1 - pair
    position = lax.broadcasted_iota(jnp.int32, (1, length), 1)
    lower = position < first
    upper = jnp.logical_and(position >= first, position < TRUNC + 2)
    offset = jnp.where(lower, position, position - first)
    odd = offset % 2 == 1
    zero = jnp.zeros_like(basis)
    signed = jnp.where(odd, -basis, basis)
    rows_ref[0:half, :] = jnp.where(lower, basis, zero)
    rows_ref[half : 2 * half, :] = jnp.where(lower, signed, zero)
    rows_ref[2 * half : 3 * half, :] = jnp.where(upper, basis, zero)
    rows_ref[3 * half : 4 * half, :] = jnp.where(upper, signed, zero)


def synth_kernel(ids_ref, spec_ref, basis_ref, out_ref, rows_ref):
    block = basis_ref.shape[0]
    step = pl.program_id(0)
    for i in range(block):
        masked_rows(ids_ref, step * block + i, basis_ref[i], rows_ref)
        out = lax.dot_general(
            rows_ref[...], spec_ref[i], (((1,), (1,)), ((), ())),
            preferred_element_type=jnp.float32,
        )
        out_ref[i] = out.astype(out_ref.dtype)


def analyse_kernel(ids_ref, grad_ref, basis_ref, out_ref, rows_ref):
    block = basis_ref.shape[0]
    step = pl.program_id(0)
    for i in range(block):
        masked_rows(ids_ref, step * block + i, basis_ref[i], rows_ref)
        out = jnp.dot(grad_ref[i], rows_ref[...], preferred_element_type=jnp.float32)
        out_ref[i] = out.astype(out_ref.dtype)


def pair_block(count):
    for size in (16, 8, 4, 2, 1):
        if count % size == 0:
            return size


def synthesis(local_ids, spectral, lat_basis):
    pairs, width, length = spectral.shape
    half = lat_basis.shape[1]
    block = pair_block(pairs)
    spec = pltpu.PrefetchScalarGridSpec(
        num_scalar_prefetch=1,
        grid=(pairs // block,),
        in_specs=[
            pl.BlockSpec((block, width, length), lambda s, ids: (s, 0, 0)),
            pl.BlockSpec((block, half, length), lambda s, ids: (s, 0, 0)),
        ],
        out_specs=pl.BlockSpec((block, 4 * half, width), lambda s, ids: (s, 0, 0)),
        scratch_shapes=[pltpu.VMEM((4 * half, length), lat_basis.dtype)],
    )
    return pl.pallas_call(
        synth_kernel,
        grid_spec=spec,
        out_shape=jax.ShapeDtypeStruct((pairs, 4 * half, width), jnp.bfloat16),
    )(local_ids, spectral, lat_basis)


def analysis(local_ids, grads, lat_basis):
    pairs, width, rows = grads.shape
    half, length = lat_basis.shape[1], lat_basis.shape[2]
    block = pair_block(pairs)
    spec = pltpu.PrefetchScalarGridSpec(
        num_scalar_prefetch=1,
        grid=(pairs // block,),
        in_specs=[
            pl.BlockSpec((block, width, rows), lambda s, ids: (s, 0, 0)),
            pl.BlockSpec((block, half, length), lambda s, ids: (s, 0, 0)),
        ],
        out_specs=pl.BlockSpec((block, width, length), lambda s, ids: (s, 0, 0)),
        scratch_shapes=[pltpu.VMEM((4 * half, length), lat_basis.dtype)],
    )
    return pl.pallas_call(
        analyse_kernel,
        grid_spec=spec,
        out_shape=jax.ShapeDtypeStruct((pairs, width, length), jnp.bfloat16),
    )(local_ids, grads, lat_basis)


def per_device(
    pair_table, spectral, lat_basis, in_weight, in_bias, out_weight, out_bias, cotangent
):
    pair_dev = spectral.shape[0]
    width_local = spectral.shape[1]
    lat_half = lat_basis.shape[1]
    band_rows = cotangent.shape[0]
    block_cols = cotangent.shape[2]
    lon_total = block_cols * lax.axis_size("lon")
    first_row = lax.axis_index("lat") * pair_dev
    local_ids = lax.dynamic_slice_in_dim(pair_table, first_row, pair_dev)
    lat_window = 2 * lat_half
    raw_waves = synthesis(local_ids, spectral, lat_basis).reshape(
        pair_dev, 2, lat_window, width_local
    )
    lat_index = jnp.arange(lat_window, dtype=jnp.int32)
    kernel_row = jnp.where(lat_index < lat_half, lat_index, 3 * lat_half - 1 - lat_index)
    reorder = (kernel_row[:, None] == lat_index[None, :]).astype(jnp.bfloat16)
    waves = jnp.einsum(
        "lr,pqrk->pqlk", reorder, raw_waves, preferred_element_type=jnp.float32
    ).astype(jnp.bfloat16)
    wave_count = 2 * pair_dev * lax.axis_size("lat")
    numbers = wave_numbers(pair_table)
    full_table = fourier_table(numbers, lon_total)
    lon_parts = lax.axis_size("lon")
    block_table = full_table.reshape(2, wave_count, lon_parts, block_cols)
    halves = 2 if width_local % 4 == 0 else 1
    chunk = width_local // halves
    pieces = []
    for h in range(halves):
        flat_waves = waves[..., h * chunk : (h + 1) * chunk].reshape(
            2 * pair_dev, lat_window * chunk
        )
        band_waves = lax.all_to_all(flat_waves, "lat", split_axis=1, concat_axis=0, tiled=True)
        coeff_grid = band_waves.reshape(wave_count, band_rows, chunk // 2, 2)
        all_columns = jnp.einsum(
            "glkc,cgbn->blkn", coeff_grid, block_table, preferred_element_type=jnp.float32
        ).astype(jnp.bfloat16)
        pieces.append(lax.all_to_all(all_columns, "lon", 0, 0, tiled=True))
    level_blocks = jnp.stack(pieces, axis=1)
    grid = jnp.transpose(level_blocks, (2, 0, 1, 3, 4)).reshape(band_rows, -1, block_cols)
    pre_act = (
        jnp.einsum("lkc,kh->lch", grid, in_weight, preferred_element_type=jnp.float32) + in_bias
    )
    activated, gelu_back = jax.vjp(jax.nn.gelu, pre_act)
    hidden = activated.astype(jnp.bfloat16)
    tendency = (
        jnp.einsum("lch,hk->lkc", hidden, out_weight, preferred_element_type=jnp.float32)
        + out_bias[None, :, None]
    ).astype(jnp.bfloat16)
    out_weight_part = jnp.einsum(
        "lch,lkc->kh", hidden, cotangent, preferred_element_type=jnp.float32
    )
    out_bias_part = jnp.sum(cotangent.astype(jnp.float32), axis=(0, 2))
    hidden_grad = jnp.einsum(
        "lkc,hk->lch", cotangent, out_weight, preferred_element_type=jnp.float32
    )
    pre_grad = gelu_back(hidden_grad)[0].astype(jnp.bfloat16)
    in_weight_part = jnp.einsum("lkc,lch->kh", grid, pre_grad, preferred_element_type=jnp.float32)
    in_bias_part = jnp.sum(pre_grad.astype(jnp.float32), axis=(0, 1))
    grid_grad = jnp.einsum(
        "lch,kh->lkc", pre_grad, in_weight, preferred_element_type=jnp.float32
    ).astype(jnp.bfloat16)
    channels, hid = in_weight.shape
    width = max(hid, channels)

    def widen(v):
        return jnp.pad(v, ((0, 0), (0, width - v.shape[1])))

    stacked = jnp.concatenate(
        [
            widen(in_weight_part),
            widen(out_weight_part),
            widen(in_bias_part[None, :]),
            widen(out_bias_part[None, :]),
        ],
        axis=0,
    )
    summed = all_reduce(stacked, ("lat", "lon"))
    in_weight_grad = summed[:channels, :hid]
    out_weight_grad = summed[channels : 2 * channels, :hid].T
    in_bias_grad = summed[2 * channels, :hid]
    out_bias_grad = summed[2 * channels + 1, :channels]
    grad_blocks = jnp.swapaxes(grid_grad.reshape(band_rows, lon_parts, -1, block_cols), 0, 1)
    level_rows = lax.all_to_all(grad_blocks, "lon", 0, 0, tiled=True)
    wave_grad = jnp.einsum(
        "cgbn,blkn->glkc", block_table, level_rows, preferred_element_type=jnp.float32
    ).astype(jnp.bfloat16)
    flat_grad = wave_grad.reshape(wave_count, band_rows * width_local)
    pair_grad = lax.all_to_all(flat_grad, "lat", split_axis=0, concat_axis=1, tiled=True)
    pair_grad = pair_grad.reshape(pair_dev, 2, lat_window, width_local)
    pair_grad = jnp.einsum(
        "lr,pqlk->pkqr", reorder, pair_grad, preferred_element_type=jnp.float32
    ).astype(jnp.bfloat16).reshape(pair_dev, width_local, 2 * lat_window)
    spectral_grad = analysis(local_ids, pair_grad, lat_basis)
    return (tendency, spectral_grad, in_weight_grad, in_bias_grad, out_weight_grad, out_bias_grad)


def solution(mesh):
    placed = (
        P(),
        P("lat", "lon", None),
        P("lat", None, None),
        P(),
        P(),
        P(),
        P(),
        P("lat", None, "lon"),
    )
    return jax.shard_map(
        per_device,
        mesh=mesh,
        in_specs=placed,
        out_specs=(P("lat", None, "lon"), P("lat", "lon", None), P(), P(), P(), P()),
        check_vma=False,
    )
```

```python
import math

import jax
import jax.numpy as jnp
from jax import lax
from jax.experimental import pallas as pl
from jax.experimental.pallas import tpu as pltpu
from jax.sharding import PartitionSpec as P

TRUNC = 1279


def pair_masks(pair_ids, length):
    first_len = TRUNC + 1 - pair_ids
    position = jnp.arange(length, dtype=jnp.int32)[None, :]
    lower_part = position < first_len[:, None]
    upper_part = jnp.logical_and(position >= first_len[:, None], position < TRUNC + 2)
    offset = jnp.where(lower_part, position, position - first_len[:, None])
    parity = jnp.where(offset % 2 == 0, 1.0, -1.0).astype(jnp.float32)
    return (lower_part, upper_part, parity, first_len)


def wave_numbers(pair_ids):
    both = jnp.stack([pair_ids, TRUNC - pair_ids], axis=1)
    return both.reshape(-1)


def table_kernel(cos_a_ref, sin_a_ref, cos_b_ref, sin_b_ref, factor_ref, out_ref):
    fine = cos_b_ref.shape[1]
    cos_b = cos_b_ref[...]
    sin_b = sin_b_ref[...]
    factor = factor_ref[...]
    for u in range(cos_a_ref.shape[1]):
        cos_a = cos_a_ref[:, u : u + 1]
        sin_a = sin_a_ref[:, u : u + 1]
        cols = slice(u * fine, (u + 1) * fine)
        out_ref[0, :, cols] = (factor * (cos_a * cos_b - sin_a * sin_b)).astype(out_ref.dtype)
        out_ref[1, :, cols] = (-factor * (sin_a * cos_b + cos_a * sin_b)).astype(out_ref.dtype)


def fourier_table(numbers, lon_total):
    fine = 128
    count = numbers.shape[0]
    coarse = jnp.arange(lon_total // fine, dtype=jnp.int32) * fine
    scale = 2.0 * math.pi / lon_total

    def angles(offsets):
        phase = numbers[:, None] * offsets[None, :] % lon_total
        angle = phase.astype(jnp.float32) * scale
        return jnp.cos(angle), jnp.sin(angle)

    cos_a, sin_a = angles(coarse)
    cos_b, sin_b = angles(jnp.arange(fine, dtype=jnp.int32))
    factor = jnp.where(numbers == 0, 1.0, 2.0).astype(jnp.float32)[:, None]
    rows = 128 if count % 128 == 0 else count
    return pl.pallas_call(
        table_kernel,
        grid=(count // rows,),
        in_specs=[
            pl.BlockSpec((rows, coarse.shape[0]), lambda i: (i, 0)),
            pl.BlockSpec((rows, coarse.shape[0]), lambda i: (i, 0)),
            pl.BlockSpec((rows, fine), lambda i: (i, 0)),
            pl.BlockSpec((rows, fine), lambda i: (i, 0)),
            pl.BlockSpec((rows, 1), lambda i: (i, 0)),
        ],
        out_specs=pl.BlockSpec((2, rows, lon_total), lambda i: (0, i, 0)),
        out_shape=jax.ShapeDtypeStruct((2, count, lon_total), jnp.bfloat16),
    )(cos_a, sin_a, cos_b, sin_b, factor)


def all_reduce(value, axes):
    count = 1
    for name in axes:
        count *= lax.axis_size(name)
    flat = value.reshape(-1)
    chunk = -(-flat.shape[0] // (count * 128)) * 128
    flat = jnp.pad(flat, (0, chunk * count - flat.shape[0]))
    sent = flat.reshape(count, chunk).astype(jnp.bfloat16)
    parts = lax.all_to_all(sent, axes, 0, 0, tiled=True)
    owned = jnp.sum(parts.astype(jnp.float32), axis=0, keepdims=True)
    spread = jnp.broadcast_to(owned, (count, chunk))
    whole = lax.all_to_all(spread, axes, 0, 0, tiled=True).reshape(-1)
    return whole[: value.size].reshape(value.shape)


def masked_rows(ids_ref, pair_index, basis, rows_ref):
    half, length = basis.shape
    pair = ids_ref[pair_index]
    first = TRUNC + 1 - pair
    position = lax.broadcasted_iota(jnp.int32, (1, length), 1)
    lower = position < first
    upper = jnp.logical_and(position >= first, position < TRUNC + 2)
    offset = jnp.where(lower, position, position - first)
    odd = offset % 2 == 1
    zero = jnp.zeros_like(basis)
    signed = jnp.where(odd, -basis, basis)
    rows_ref[0:half, :] = jnp.where(lower, basis, zero)
    rows_ref[half : 2 * half, :] = jnp.where(lower, signed, zero)
    rows_ref[2 * half : 3 * half, :] = jnp.where(upper, basis, zero)
    rows_ref[3 * half : 4 * half, :] = jnp.where(upper, signed, zero)


def synth_kernel(ids_ref, spec_ref, basis_ref, out_ref, rows_ref):
    block = basis_ref.shape[0]
    step = pl.program_id(0)
    for i in range(block):
        masked_rows(ids_ref, step * block + i, basis_ref[i], rows_ref)
        out = lax.dot_general(
            rows_ref[...], spec_ref[i], (((1,), (1,)), ((), ())),
            preferred_element_type=jnp.float32,
        )
        out_ref[i] = out.astype(out_ref.dtype)


def analyse_kernel(ids_ref, grad_ref, basis_ref, out_ref, rows_ref):
    block = basis_ref.shape[0]
    step = pl.program_id(0)
    for i in range(block):
        masked_rows(ids_ref, step * block + i, basis_ref[i], rows_ref)
        out = jnp.dot(grad_ref[i], rows_ref[...], preferred_element_type=jnp.float32)
        out_ref[i] = out.astype(out_ref.dtype)


def pair_block(count):
    for size in (16, 8, 4, 2, 1):
        if count % size == 0:
            return size


def synthesis(local_ids, spectral, lat_basis):
    pairs, width, length = spectral.shape
    half = lat_basis.shape[1]
    block = pair_block(pairs)
    spec = pltpu.PrefetchScalarGridSpec(
        num_scalar_prefetch=1,
        grid=(pairs // block,),
        in_specs=[
            pl.BlockSpec((block, width, length), lambda s, ids: (s, 0, 0)),
            pl.BlockSpec((block, half, length), lambda s, ids: (s, 0, 0)),
        ],
        out_specs=pl.BlockSpec((block, 4 * half, width), lambda s, ids: (s, 0, 0)),
        scratch_shapes=[pltpu.VMEM((4 * half, length), lat_basis.dtype)],
    )
    return pl.pallas_call(
        synth_kernel,
        grid_spec=spec,
        out_shape=jax.ShapeDtypeStruct((pairs, 4 * half, width), jnp.bfloat16),
    )(local_ids, spectral, lat_basis)


def analysis(local_ids, grads, lat_basis):
    pairs, width, rows = grads.shape
    half, length = lat_basis.shape[1], lat_basis.shape[2]
    block = pair_block(pairs)
    spec = pltpu.PrefetchScalarGridSpec(
        num_scalar_prefetch=1,
        grid=(pairs // block,),
        in_specs=[
            pl.BlockSpec((block, width, rows), lambda s, ids: (s, 0, 0)),
            pl.BlockSpec((block, half, length), lambda s, ids: (s, 0, 0)),
        ],
        out_specs=pl.BlockSpec((block, width, length), lambda s, ids: (s, 0, 0)),
        scratch_shapes=[pltpu.VMEM((4 * half, length), lat_basis.dtype)],
    )
    return pl.pallas_call(
        analyse_kernel,
        grid_spec=spec,
        out_shape=jax.ShapeDtypeStruct((pairs, width, length), jnp.bfloat16),
    )(local_ids, grads, lat_basis)


def per_device(
    pair_table, spectral, lat_basis, in_weight, in_bias, out_weight, out_bias, cotangent
):
    pair_dev = spectral.shape[0]
    width_local = spectral.shape[1]
    lat_half = lat_basis.shape[1]
    band_rows = cotangent.shape[0]
    block_cols = cotangent.shape[2]
    lon_total = block_cols * lax.axis_size("lon")
    first_row = lax.axis_index("lat") * pair_dev
    local_ids = lax.dynamic_slice_in_dim(pair_table, first_row, pair_dev)
    lat_window = 2 * lat_half
    raw_waves = synthesis(local_ids, spectral, lat_basis).reshape(
        pair_dev, 2, lat_window, width_local
    )
    lat_index = jnp.arange(lat_window, dtype=jnp.int32)
    kernel_row = jnp.where(lat_index < lat_half, lat_index, 3 * lat_half - 1 - lat_index)
    reorder = (kernel_row[:, None] == lat_index[None, :]).astype(jnp.bfloat16)
    waves = jnp.einsum(
        "lr,pqrk->pqlk", reorder, raw_waves, preferred_element_type=jnp.float32
    ).astype(jnp.bfloat16)
    flat_waves = waves.reshape(2 * pair_dev, lat_window * width_local)
    band_waves = lax.all_to_all(flat_waves, "lat", split_axis=1, concat_axis=0, tiled=True)
    wave_count = band_waves.shape[0]
    coeff_grid = band_waves.reshape(wave_count, band_rows, width_local // 2, 2)
    numbers = wave_numbers(pair_table)
    full_table = fourier_table(numbers, lon_total)
    lon_parts = lax.axis_size("lon")
    block_table = full_table.reshape(2, wave_count, lon_parts, block_cols)
    all_columns = jnp.einsum(
        "glkc,cgbn->blkn", coeff_grid, block_table, preferred_element_type=jnp.float32
    ).astype(jnp.bfloat16)
    level_blocks = lax.all_to_all(all_columns, "lon", 0, 0, tiled=True)
    grid = jnp.swapaxes(level_blocks, 0, 1).reshape(band_rows, -1, block_cols)
    pre_act = (
        jnp.einsum("lkc,kh->lch", grid, in_weight, preferred_element_type=jnp.float32) + in_bias
    )
    activated, gelu_back = jax.vjp(jax.nn.gelu, pre_act)
    hidden = activated.astype(jnp.bfloat16)
    tendency = (
        jnp.einsum("lch,hk->lkc", hidden, out_weight, preferred_element_type=jnp.float32)
        + out_bias[None, :, None]
    ).astype(jnp.bfloat16)
    out_weight_part = jnp.einsum(
        "lch,lkc->kh", hidden, cotangent, preferred_element_type=jnp.float32
    )
    out_bias_part = jnp.sum(cotangent.astype(jnp.float32), axis=(0, 2))
    hidden_grad = jnp.einsum(
        "lkc,hk->lch", cotangent, out_weight, preferred_element_type=jnp.float32
    )
    pre_grad = gelu_back(hidden_grad)[0].astype(jnp.bfloat16)
    in_weight_part = jnp.einsum("lkc,lch->kh", grid, pre_grad, preferred_element_type=jnp.float32)
    in_bias_part = jnp.sum(pre_grad.astype(jnp.float32), axis=(0, 1))
    grid_grad = jnp.einsum(
        "lch,kh->lkc", pre_grad, in_weight, preferred_element_type=jnp.float32
    ).astype(jnp.bfloat16)
    channels, hid = in_weight.shape
    width = max(hid, channels)

    def widen(v):
        return jnp.pad(v, ((0, 0), (0, width - v.shape[1])))

    stacked = jnp.concatenate(
        [
            widen(in_weight_part),
            widen(out_weight_part),
            widen(in_bias_part[None, :]),
            widen(out_bias_part[None, :]),
        ],
        axis=0,
    )
    grad_blocks = jnp.swapaxes(grid_grad.reshape(band_rows, lon_parts, -1, block_cols), 0, 1)
    level_rows = lax.all_to_all(grad_blocks, "lon", 0, 0, tiled=True)
    stacked, level_rows = lax.optimization_barrier((stacked, level_rows))
    summed = all_reduce(stacked, ("lat", "lon"))
    in_weight_grad = summed[:channels, :hid]
    out_weight_grad = summed[channels : 2 * channels, :hid].T
    in_bias_grad = summed[2 * channels, :hid]
    out_bias_grad = summed[2 * channels + 1, :channels]
    wave_grad = jnp.einsum(
        "cgbn,blkn->glkc", block_table, level_rows, preferred_element_type=jnp.float32
    ).astype(jnp.bfloat16)
    flat_grad = wave_grad.reshape(wave_count, band_rows * width_local)
    pair_grad = lax.all_to_all(flat_grad, "lat", split_axis=0, concat_axis=1, tiled=True)
    pair_grad = pair_grad.reshape(pair_dev, 2, lat_window, width_local)
    pair_grad = jnp.einsum(
        "lr,pqlk->pkqr", reorder, pair_grad, preferred_element_type=jnp.float32
    ).astype(jnp.bfloat16).reshape(pair_dev, width_local, 2 * lat_window)
    spectral_grad = analysis(local_ids, pair_grad, lat_basis)
    return (tendency, spectral_grad, in_weight_grad, in_bias_grad, out_weight_grad, out_bias_grad)


def solution(mesh):
    placed = (
        P(),
        P("lat", "lon", None),
        P("lat", None, None),
        P(),
        P(),
        P(),
        P(),
        P("lat", None, "lon"),
    )
    return jax.shard_map(
        per_device,
        mesh=mesh,
        in_specs=placed,
        out_specs=(P("lat", None, "lon"), P("lat", "lon", None), P(), P(), P(), P()),
        check_vma=False,
    )
```

```python
import math

import jax
import jax.numpy as jnp
from jax import lax
from jax.experimental import pallas as pl
from jax.experimental.pallas import tpu as pltpu
from jax.sharding import PartitionSpec as P

TRUNC = 1279


def pair_masks(pair_ids, length):
    first_len = TRUNC + 1 - pair_ids
    position = jnp.arange(length, dtype=jnp.int32)[None, :]
    lower_part = position < first_len[:, None]
    upper_part = jnp.logical_and(position >= first_len[:, None], position < TRUNC + 2)
    offset = jnp.where(lower_part, position, position - first_len[:, None])
    parity = jnp.where(offset % 2 == 0, 1.0, -1.0).astype(jnp.float32)
    return (lower_part, upper_part, parity, first_len)


def wave_numbers(pair_ids):
    both = jnp.stack([pair_ids, TRUNC - pair_ids], axis=1)
    return both.reshape(-1)


def table_kernel(cos_a_ref, sin_a_ref, cos_b_ref, sin_b_ref, factor_ref, out_ref):
    fine = cos_b_ref.shape[1]
    cos_b = cos_b_ref[...]
    sin_b = sin_b_ref[...]
    factor = factor_ref[...]
    for u in range(cos_a_ref.shape[1]):
        cos_a = cos_a_ref[:, u : u + 1]
        sin_a = sin_a_ref[:, u : u + 1]
        cols = slice(u * fine, (u + 1) * fine)
        out_ref[0, :, cols] = (factor * (cos_a * cos_b - sin_a * sin_b)).astype(out_ref.dtype)
        out_ref[1, :, cols] = (-factor * (sin_a * cos_b + cos_a * sin_b)).astype(out_ref.dtype)


def fourier_table(numbers, lon_total):
    fine = 128
    count = numbers.shape[0]
    coarse = jnp.arange(lon_total // fine, dtype=jnp.int32) * fine
    scale = 2.0 * math.pi / lon_total

    def angles(offsets):
        phase = numbers[:, None] * offsets[None, :] % lon_total
        angle = phase.astype(jnp.float32) * scale
        return jnp.cos(angle), jnp.sin(angle)

    cos_a, sin_a = angles(coarse)
    cos_b, sin_b = angles(jnp.arange(fine, dtype=jnp.int32))
    factor = jnp.where(numbers == 0, 1.0, 2.0).astype(jnp.float32)[:, None]
    rows = 128 if count % 128 == 0 else count
    return pl.pallas_call(
        table_kernel,
        grid=(count // rows,),
        in_specs=[
            pl.BlockSpec((rows, coarse.shape[0]), lambda i: (i, 0)),
            pl.BlockSpec((rows, coarse.shape[0]), lambda i: (i, 0)),
            pl.BlockSpec((rows, fine), lambda i: (i, 0)),
            pl.BlockSpec((rows, fine), lambda i: (i, 0)),
            pl.BlockSpec((rows, 1), lambda i: (i, 0)),
        ],
        out_specs=pl.BlockSpec((2, rows, lon_total), lambda i: (0, i, 0)),
        out_shape=jax.ShapeDtypeStruct((2, count, lon_total), jnp.bfloat16),
    )(cos_a, sin_a, cos_b, sin_b, factor)


def all_reduce(value, axes):
    count = 1
    for name in axes:
        count *= lax.axis_size(name)
    flat = value.reshape(-1)
    chunk = -(-flat.shape[0] // (count * 128)) * 128
    flat = jnp.pad(flat, (0, chunk * count - flat.shape[0]))
    sent = flat.reshape(count, chunk).astype(jnp.bfloat16)
    parts = lax.all_to_all(sent, axes, 0, 0, tiled=True)
    owned = jnp.sum(parts.astype(jnp.float32), axis=0, keepdims=True)
    spread = jnp.broadcast_to(owned, (count, chunk))
    whole = lax.all_to_all(spread, axes, 0, 0, tiled=True).reshape(-1)
    return whole[: value.size].reshape(value.shape)


def masked_rows(ids_ref, pair_index, basis, rows_ref):
    half, length = basis.shape
    pair = ids_ref[pair_index]
    first = TRUNC + 1 - pair
    position = lax.broadcasted_iota(jnp.int32, (1, length), 1)
    lower = position < first
    upper = jnp.logical_and(position >= first, position < TRUNC + 2)
    offset = jnp.where(lower, position, position - first)
    odd = offset % 2 == 1
    zero = jnp.zeros_like(basis)
    signed = jnp.where(odd, -basis, basis)
    rows_ref[0:half, :] = jnp.where(lower, basis, zero)
    rows_ref[half : 2 * half, :] = jnp.where(lower, signed, zero)
    rows_ref[2 * half : 3 * half, :] = jnp.where(upper, basis, zero)
    rows_ref[3 * half : 4 * half, :] = jnp.where(upper, signed, zero)


def synth_kernel(ids_ref, spec_ref, basis_ref, out_ref, rows_ref):
    block = basis_ref.shape[0]
    step = pl.program_id(0)
    for i in range(block):
        masked_rows(ids_ref, step * block + i, basis_ref[i], rows_ref)
        out = lax.dot_general(
            rows_ref[...], spec_ref[i], (((1,), (1,)), ((), ())),
            preferred_element_type=jnp.float32,
        )
        out_ref[i] = out.astype(out_ref.dtype)


def analyse_kernel(ids_ref, grad_ref, basis_ref, out_ref, rows_ref):
    block = basis_ref.shape[0]
    step = pl.program_id(0)
    for i in range(block):
        masked_rows(ids_ref, step * block + i, basis_ref[i], rows_ref)
        out = lax.dot_general(
            grad_ref[i], rows_ref[...], (((0,), (0,)), ((), ())),
            preferred_element_type=jnp.float32,
        )
        out_ref[i] = out.astype(out_ref.dtype)


def pair_block(count):
    for size in (16, 8, 4, 2, 1):
        if count % size == 0:
            return size


def synthesis(local_ids, spectral, lat_basis):
    pairs, width, length = spectral.shape
    half = lat_basis.shape[1]
    block = pair_block(pairs)
    spec = pltpu.PrefetchScalarGridSpec(
        num_scalar_prefetch=1,
        grid=(pairs // block,),
        in_specs=[
            pl.BlockSpec((block, width, length), lambda s, ids: (s, 0, 0)),
            pl.BlockSpec((block, half, length), lambda s, ids: (s, 0, 0)),
        ],
        out_specs=pl.BlockSpec((block, 4 * half, width), lambda s, ids: (s, 0, 0)),
        scratch_shapes=[pltpu.VMEM((4 * half, length), lat_basis.dtype)],
    )
    return pl.pallas_call(
        synth_kernel,
        grid_spec=spec,
        out_shape=jax.ShapeDtypeStruct((pairs, 4 * half, width), jnp.bfloat16),
    )(local_ids, spectral, lat_basis)


def analysis(local_ids, grads, lat_basis):
    pairs, rows, width = grads.shape
    half, length = lat_basis.shape[1], lat_basis.shape[2]
    block = pair_block(pairs)
    spec = pltpu.PrefetchScalarGridSpec(
        num_scalar_prefetch=1,
        grid=(pairs // block,),
        in_specs=[
            pl.BlockSpec((block, rows, width), lambda s, ids: (s, 0, 0)),
            pl.BlockSpec((block, half, length), lambda s, ids: (s, 0, 0)),
        ],
        out_specs=pl.BlockSpec((block, width, length), lambda s, ids: (s, 0, 0)),
        scratch_shapes=[pltpu.VMEM((4 * half, length), lat_basis.dtype)],
    )
    return pl.pallas_call(
        analyse_kernel,
        grid_spec=spec,
        out_shape=jax.ShapeDtypeStruct((pairs, width, length), jnp.bfloat16),
    )(local_ids, grads, lat_basis)


def per_device(
    pair_table, spectral, lat_basis, in_weight, in_bias, out_weight, out_bias, cotangent
):
    pair_dev = spectral.shape[0]
    width_local = spectral.shape[1]
    lat_half = lat_basis.shape[1]
    band_rows = cotangent.shape[0]
    block_cols = cotangent.shape[2]
    lon_total = block_cols * lax.axis_size("lon")
    first_row = lax.axis_index("lat") * pair_dev
    local_ids = lax.dynamic_slice_in_dim(pair_table, first_row, pair_dev)
    lat_window = 2 * lat_half
    raw_waves = synthesis(local_ids, spectral, lat_basis).reshape(
        pair_dev, 2, lat_window, width_local
    )
    lat_index = jnp.arange(lat_window, dtype=jnp.int32)
    kernel_row = jnp.where(lat_index < lat_half, lat_index, 3 * lat_half - 1 - lat_index)
    reorder = (kernel_row[:, None] == lat_index[None, :]).astype(jnp.bfloat16)
    waves = jnp.einsum(
        "lr,pqrk->pqlk", reorder, raw_waves, preferred_element_type=jnp.float32
    ).astype(jnp.bfloat16)
    flat_waves = waves.reshape(2 * pair_dev, lat_window * width_local)
    band_waves = lax.all_to_all(flat_waves, "lat", split_axis=1, concat_axis=0, tiled=True)
    wave_count = band_waves.shape[0]
    coeff_grid = band_waves.reshape(wave_count, band_rows, width_local // 2, 2)
    numbers = wave_numbers(pair_table)
    full_table = fourier_table(numbers, lon_total)
    lon_parts = lax.axis_size("lon")
    block_table = full_table.reshape(2, wave_count, lon_parts, block_cols)
    all_columns = jnp.einsum(
        "glkc,cgbn->blkn", coeff_grid, block_table, preferred_element_type=jnp.float32
    ).astype(jnp.bfloat16)
    level_blocks = lax.all_to_all(all_columns, "lon", 0, 0, tiled=True)
    grid = jnp.swapaxes(level_blocks, 0, 1).reshape(band_rows, -1, block_cols)
    pre_act = (
        jnp.einsum("lkc,kh->lch", grid, in_weight, preferred_element_type=jnp.float32) + in_bias
    )
    activated, gelu_back = jax.vjp(jax.nn.gelu, pre_act)
    hidden = activated.astype(jnp.bfloat16)
    tendency = (
        jnp.einsum("lch,hk->lkc", hidden, out_weight, preferred_element_type=jnp.float32)
        + out_bias[None, :, None]
    ).astype(jnp.bfloat16)
    out_weight_part = jnp.einsum(
        "lch,lkc->kh", hidden, cotangent, preferred_element_type=jnp.float32
    )
    out_bias_part = jnp.sum(cotangent.astype(jnp.float32), axis=(0, 2))
    hidden_grad = jnp.einsum(
        "lkc,hk->lch", cotangent, out_weight, preferred_element_type=jnp.float32
    )
    pre_grad = gelu_back(hidden_grad)[0].astype(jnp.bfloat16)
    in_weight_part = jnp.einsum("lkc,lch->kh", grid, pre_grad, preferred_element_type=jnp.float32)
    in_bias_part = jnp.sum(pre_grad.astype(jnp.float32), axis=(0, 1))
    grid_grad = jnp.einsum(
        "lch,kh->lkc", pre_grad, in_weight, preferred_element_type=jnp.float32
    ).astype(jnp.bfloat16)
    channels, hid = in_weight.shape
    width = max(hid, channels)

    def widen(v):
        return jnp.pad(v, ((0, 0), (0, width - v.shape[1])))

    stacked = jnp.concatenate(
        [
            widen(in_weight_part),
            widen(out_weight_part),
            widen(in_bias_part[None, :]),
            widen(out_bias_part[None, :]),
        ],
        axis=0,
    )
    summed = all_reduce(stacked, ("lat", "lon"))
    in_weight_grad = summed[:channels, :hid]
    out_weight_grad = summed[channels : 2 * channels, :hid].T
    in_bias_grad = summed[2 * channels, :hid]
    out_bias_grad = summed[2 * channels + 1, :channels]
    grad_blocks = jnp.swapaxes(grid_grad.reshape(band_rows, lon_parts, -1, block_cols), 0, 1)
    level_rows = lax.all_to_all(grad_blocks, "lon", 0, 0, tiled=True)
    wave_grad = jnp.einsum(
        "cgbn,blkn->glkc", block_table, level_rows, preferred_element_type=jnp.float32
    ).astype(jnp.bfloat16)
    flat_grad = wave_grad.reshape(wave_count, band_rows * width_local)
    pair_grad = lax.all_to_all(flat_grad, "lat", split_axis=0, concat_axis=1, tiled=True)
    pair_grad = pair_grad.reshape(pair_dev, 2, lat_window, width_local)
    pair_grad = jnp.einsum(
        "lr,pqlk->pqrk", reorder, pair_grad, preferred_element_type=jnp.float32
    ).astype(jnp.bfloat16).reshape(pair_dev, 2 * lat_window, width_local)
    spectral_grad = analysis(local_ids, pair_grad, lat_basis)
    return (tendency, spectral_grad, in_weight_grad, in_bias_grad, out_weight_grad, out_bias_grad)


def solution(mesh):
    placed = (
        P(),
        P("lat", "lon", None),
        P("lat", None, None),
        P(),
        P(),
        P(),
        P(),
        P("lat", None, "lon"),
    )
    return jax.shard_map(
        per_device,
        mesh=mesh,
        in_specs=placed,
        out_specs=(P("lat", None, "lon"), P("lat", "lon", None), P(), P(), P(), P()),
        check_vma=False,
    )
```

```python
import math

import jax
import jax.numpy as jnp
from jax import lax
from jax.experimental import pallas as pl
from jax.experimental.pallas import tpu as pltpu
from jax.sharding import PartitionSpec as P

TRUNC = 1279


def pair_masks(pair_ids, length):
    first_len = TRUNC + 1 - pair_ids
    position = jnp.arange(length, dtype=jnp.int32)[None, :]
    lower_part = position < first_len[:, None]
    upper_part = jnp.logical_and(position >= first_len[:, None], position < TRUNC + 2)
    offset = jnp.where(lower_part, position, position - first_len[:, None])
    parity = jnp.where(offset % 2 == 0, 1.0, -1.0).astype(jnp.float32)
    return (lower_part, upper_part, parity, first_len)


def wave_numbers(pair_ids):
    both = jnp.stack([pair_ids, TRUNC - pair_ids], axis=1)
    return both.reshape(-1)


def table_kernel(cos_a_ref, sin_a_ref, cos_b_ref, sin_b_ref, factor_ref, out_ref):
    fine = cos_b_ref.shape[1]
    cos_b = cos_b_ref[...]
    sin_b = sin_b_ref[...]
    factor = factor_ref[...]
    for u in range(cos_a_ref.shape[1]):
        cos_a = cos_a_ref[:, u : u + 1]
        sin_a = sin_a_ref[:, u : u + 1]
        cols = slice(u * fine, (u + 1) * fine)
        out_ref[0, :, cols] = (factor * (cos_a * cos_b - sin_a * sin_b)).astype(out_ref.dtype)
        out_ref[1, :, cols] = (-factor * (sin_a * cos_b + cos_a * sin_b)).astype(out_ref.dtype)


def fourier_table(numbers, lon_total):
    fine = 128
    count = numbers.shape[0]
    coarse = jnp.arange(lon_total // fine, dtype=jnp.int32) * fine
    scale = 2.0 * math.pi / lon_total

    def angles(offsets):
        phase = numbers[:, None] * offsets[None, :] % lon_total
        angle = phase.astype(jnp.float32) * scale
        return jnp.cos(angle), jnp.sin(angle)

    cos_a, sin_a = angles(coarse)
    cos_b, sin_b = angles(jnp.arange(fine, dtype=jnp.int32))
    factor = jnp.where(numbers == 0, 1.0, 2.0).astype(jnp.float32)[:, None]
    rows = 128 if count % 128 == 0 else count
    return pl.pallas_call(
        table_kernel,
        grid=(count // rows,),
        in_specs=[
            pl.BlockSpec((rows, coarse.shape[0]), lambda i: (i, 0)),
            pl.BlockSpec((rows, coarse.shape[0]), lambda i: (i, 0)),
            pl.BlockSpec((rows, fine), lambda i: (i, 0)),
            pl.BlockSpec((rows, fine), lambda i: (i, 0)),
            pl.BlockSpec((rows, 1), lambda i: (i, 0)),
        ],
        out_specs=pl.BlockSpec((2, rows, lon_total), lambda i: (0, i, 0)),
        out_shape=jax.ShapeDtypeStruct((2, count, lon_total), jnp.bfloat16),
    )(cos_a, sin_a, cos_b, sin_b, factor)


def all_reduce(value, axes):
    count = 1
    for name in axes:
        count *= lax.axis_size(name)
    flat = value.reshape(-1)
    chunk = -(-flat.shape[0] // (count * 128)) * 128
    flat = jnp.pad(flat, (0, chunk * count - flat.shape[0]))
    sent = flat.reshape(count, chunk).astype(jnp.bfloat16)
    parts = lax.all_to_all(sent, axes, 0, 0, tiled=True)
    owned = jnp.sum(parts.astype(jnp.float32), axis=0, keepdims=True)
    spread = jnp.broadcast_to(owned, (count, chunk))
    whole = lax.all_to_all(spread, axes, 0, 0, tiled=True).reshape(-1)
    return whole[: value.size].reshape(value.shape)


def masked_rows(ids_ref, pair_index, basis, rows_ref):
    half, length = basis.shape
    pair = ids_ref[pair_index]
    first = TRUNC + 1 - pair
    position = lax.broadcasted_iota(jnp.int32, (1, length), 1)
    lower = position < first
    upper = jnp.logical_and(position >= first, position < TRUNC + 2)
    offset = jnp.where(lower, position, position - first)
    odd = offset % 2 == 1
    zero = jnp.zeros_like(basis)
    signed = jnp.where(odd, -basis, basis)
    rows_ref[0:half, :] = jnp.where(lower, basis, zero)
    rows_ref[half : 2 * half, :] = jnp.where(lower, signed, zero)
    rows_ref[2 * half : 3 * half, :] = jnp.where(upper, basis, zero)
    rows_ref[3 * half : 4 * half, :] = jnp.where(upper, signed, zero)


def synth_kernel(ids_ref, spec_ref, basis_ref, out_ref, rows_ref):
    block = basis_ref.shape[0]
    step = pl.program_id(0)
    for i in range(block):
        masked_rows(ids_ref, step * block + i, basis_ref[i], rows_ref)
        out = lax.dot_general(
            rows_ref[...], spec_ref[i], (((1,), (1,)), ((), ())),
            preferred_element_type=jnp.float32,
        )
        out_ref[i] = out.astype(out_ref.dtype)


def analyse_kernel(ids_ref, grad_ref, basis_ref, out_ref, rows_ref):
    block = basis_ref.shape[0]
    step = pl.program_id(0)
    for i in range(block):
        masked_rows(ids_ref, step * block + i, basis_ref[i], rows_ref)
        out = lax.dot_general(
            grad_ref[i], rows_ref[...], (((0,), (0,)), ((), ())),
            preferred_element_type=jnp.float32,
        )
        out_ref[i] = out.astype(out_ref.dtype)


def pair_block(count):
    for size in (20, 16, 8, 4, 2, 1):
        if count % size == 0:
            return size


def synthesis(local_ids, spectral, lat_basis):
    pairs, width, length = spectral.shape
    half = lat_basis.shape[1]
    block = pair_block(pairs)
    spec = pltpu.PrefetchScalarGridSpec(
        num_scalar_prefetch=1,
        grid=(pairs // block,),
        in_specs=[
            pl.BlockSpec((block, width, length), lambda s, ids: (s, 0, 0)),
            pl.BlockSpec((block, half, length), lambda s, ids: (s, 0, 0)),
        ],
        out_specs=pl.BlockSpec((block, 4 * half, width), lambda s, ids: (s, 0, 0)),
        scratch_shapes=[pltpu.VMEM((4 * half, length), lat_basis.dtype)],
    )
    return pl.pallas_call(
        synth_kernel,
        grid_spec=spec,
        out_shape=jax.ShapeDtypeStruct((pairs, 4 * half, width), jnp.bfloat16),
    )(local_ids, spectral, lat_basis)


def analysis(local_ids, grads, lat_basis):
    pairs, rows, width = grads.shape
    half, length = lat_basis.shape[1], lat_basis.shape[2]
    block = pair_block(pairs)
    spec = pltpu.PrefetchScalarGridSpec(
        num_scalar_prefetch=1,
        grid=(pairs // block,),
        in_specs=[
            pl.BlockSpec((block, rows, width), lambda s, ids: (s, 0, 0)),
            pl.BlockSpec((block, half, length), lambda s, ids: (s, 0, 0)),
        ],
        out_specs=pl.BlockSpec((block, width, length), lambda s, ids: (s, 0, 0)),
        scratch_shapes=[pltpu.VMEM((4 * half, length), lat_basis.dtype)],
    )
    return pl.pallas_call(
        analyse_kernel,
        grid_spec=spec,
        out_shape=jax.ShapeDtypeStruct((pairs, width, length), jnp.bfloat16),
    )(local_ids, grads, lat_basis)


def per_device(
    pair_table, spectral, lat_basis, in_weight, in_bias, out_weight, out_bias, cotangent
):
    pair_dev = spectral.shape[0]
    width_local = spectral.shape[1]
    lat_half = lat_basis.shape[1]
    band_rows = cotangent.shape[0]
    block_cols = cotangent.shape[2]
    lon_total = block_cols * lax.axis_size("lon")
    first_row = lax.axis_index("lat") * pair_dev
    local_ids = lax.dynamic_slice_in_dim(pair_table, first_row, pair_dev)
    lat_window = 2 * lat_half
    raw_waves = synthesis(local_ids, spectral, lat_basis).reshape(
        pair_dev, 2, lat_window, width_local
    )
    lat_index = jnp.arange(lat_window, dtype=jnp.int32)
    kernel_row = jnp.where(lat_index < lat_half, lat_index, 3 * lat_half - 1 - lat_index)
    reorder = (kernel_row[:, None] == lat_index[None, :]).astype(jnp.bfloat16)
    waves = jnp.einsum(
        "lr,pqrk->pqlk", reorder, raw_waves, preferred_element_type=jnp.float32
    ).astype(jnp.bfloat16)
    flat_waves = waves.reshape(2 * pair_dev, lat_window * width_local)
    band_waves = lax.all_to_all(flat_waves, "lat", split_axis=1, concat_axis=0, tiled=True)
    wave_count = band_waves.shape[0]
    coeff_grid = band_waves.reshape(wave_count, band_rows, width_local // 2, 2)
    numbers = wave_numbers(pair_table)
    full_table = fourier_table(numbers, lon_total)
    lon_parts = lax.axis_size("lon")
    block_table = full_table.reshape(2, wave_count, lon_parts, block_cols)
    all_columns = jnp.einsum(
        "glkc,cgbn->blkn", coeff_grid, block_table, preferred_element_type=jnp.float32
    ).astype(jnp.bfloat16)
    level_blocks = lax.all_to_all(all_columns, "lon", 0, 0, tiled=True)
    grid = jnp.swapaxes(level_blocks, 0, 1).reshape(band_rows, -1, block_cols)
    pre_act = (
        jnp.einsum("lkc,kh->lch", grid, in_weight, preferred_element_type=jnp.float32) + in_bias
    )
    activated, gelu_back = jax.vjp(jax.nn.gelu, pre_act)
    hidden = activated.astype(jnp.bfloat16)
    tendency = (
        jnp.einsum("lch,hk->lkc", hidden, out_weight, preferred_element_type=jnp.float32)
        + out_bias[None, :, None]
    ).astype(jnp.bfloat16)
    out_weight_part = jnp.einsum(
        "lch,lkc->kh", hidden, cotangent, preferred_element_type=jnp.float32
    )
    out_bias_part = jnp.sum(cotangent.astype(jnp.float32), axis=(0, 2))
    hidden_grad = jnp.einsum(
        "lkc,hk->lch", cotangent, out_weight, preferred_element_type=jnp.float32
    )
    pre_grad = gelu_back(hidden_grad)[0].astype(jnp.bfloat16)
    in_weight_part = jnp.einsum("lkc,lch->kh", grid, pre_grad, preferred_element_type=jnp.float32)
    in_bias_part = jnp.sum(pre_grad.astype(jnp.float32), axis=(0, 1))
    grid_grad = jnp.einsum(
        "lch,kh->lkc", pre_grad, in_weight, preferred_element_type=jnp.float32
    ).astype(jnp.bfloat16)
    channels, hid = in_weight.shape
    width = max(hid, channels)

    def widen(v):
        return jnp.pad(v, ((0, 0), (0, width - v.shape[1])))

    stacked = jnp.concatenate(
        [
            widen(in_weight_part),
            widen(out_weight_part),
            widen(in_bias_part[None, :]),
            widen(out_bias_part[None, :]),
        ],
        axis=0,
    )
    summed = all_reduce(stacked, ("lat", "lon"))
    in_weight_grad = summed[:channels, :hid]
    out_weight_grad = summed[channels : 2 * channels, :hid].T
    in_bias_grad = summed[2 * channels, :hid]
    out_bias_grad = summed[2 * channels + 1, :channels]
    grad_blocks = jnp.swapaxes(grid_grad.reshape(band_rows, lon_parts, -1, block_cols), 0, 1)
    level_rows = lax.all_to_all(grad_blocks, "lon", 0, 0, tiled=True)
    wave_grad = jnp.einsum(
        "cgbn,blkn->glkc", block_table, level_rows, preferred_element_type=jnp.float32
    ).astype(jnp.bfloat16)
    flat_grad = wave_grad.reshape(wave_count, band_rows * width_local)
    pair_grad = lax.all_to_all(flat_grad, "lat", split_axis=0, concat_axis=1, tiled=True)
    pair_grad = pair_grad.reshape(pair_dev, 2, lat_window, width_local)
    pair_grad = jnp.einsum(
        "lr,pqlk->pqrk", reorder, pair_grad, preferred_element_type=jnp.float32
    ).astype(jnp.bfloat16).reshape(pair_dev, 2 * lat_window, width_local)
    spectral_grad = analysis(local_ids, pair_grad, lat_basis)
    return (tendency, spectral_grad, in_weight_grad, in_bias_grad, out_weight_grad, out_bias_grad)


def solution(mesh):
    placed = (
        P(),
        P("lat", "lon", None),
        P("lat", None, None),
        P(),
        P(),
        P(),
        P(),
        P("lat", None, "lon"),
    )
    return jax.shard_map(
        per_device,
        mesh=mesh,
        in_specs=placed,
        out_specs=(P("lat", None, "lon"), P("lat", "lon", None), P(), P(), P(), P()),
        check_vma=False,
    )
```

```python
import math

import jax
import jax.numpy as jnp
from jax import lax
from jax.experimental import pallas as pl
from jax.experimental.pallas import tpu as pltpu
from jax.sharding import PartitionSpec as P

TRUNC = 1279


def pair_masks(pair_ids, length):
    first_len = TRUNC + 1 - pair_ids
    position = jnp.arange(length, dtype=jnp.int32)[None, :]
    lower_part = position < first_len[:, None]
    upper_part = jnp.logical_and(position >= first_len[:, None], position < TRUNC + 2)
    offset = jnp.where(lower_part, position, position - first_len[:, None])
    parity = jnp.where(offset % 2 == 0, 1.0, -1.0).astype(jnp.float32)
    return (lower_part, upper_part, parity, first_len)


def wave_numbers(pair_ids):
    both = jnp.stack([pair_ids, TRUNC - pair_ids], axis=1)
    return both.reshape(-1)


def table_kernel(cos_a_ref, sin_a_ref, cos_b_ref, sin_b_ref, factor_ref, out_ref):
    fine = cos_b_ref.shape[1]
    cos_b = cos_b_ref[...]
    sin_b = sin_b_ref[...]
    factor = factor_ref[...]
    for u in range(cos_a_ref.shape[1]):
        cos_a = cos_a_ref[:, u : u + 1]
        sin_a = sin_a_ref[:, u : u + 1]
        cols = slice(u * fine, (u + 1) * fine)
        out_ref[0, :, cols] = (factor * (cos_a * cos_b - sin_a * sin_b)).astype(out_ref.dtype)
        out_ref[1, :, cols] = (-factor * (sin_a * cos_b + cos_a * sin_b)).astype(out_ref.dtype)


def fourier_table(numbers, lon_total):
    fine = 128
    count = numbers.shape[0]
    coarse = jnp.arange(lon_total // fine, dtype=jnp.int32) * fine
    scale = 2.0 * math.pi / lon_total

    def angles(offsets):
        phase = numbers[:, None] * offsets[None, :] % lon_total
        angle = phase.astype(jnp.float32) * scale
        return jnp.cos(angle), jnp.sin(angle)

    cos_a, sin_a = angles(coarse)
    cos_b, sin_b = angles(jnp.arange(fine, dtype=jnp.int32))
    factor = jnp.where(numbers == 0, 1.0, 2.0).astype(jnp.float32)[:, None]
    rows = 128 if count % 128 == 0 else count
    return pl.pallas_call(
        table_kernel,
        grid=(count // rows,),
        in_specs=[
            pl.BlockSpec((rows, coarse.shape[0]), lambda i: (i, 0)),
            pl.BlockSpec((rows, coarse.shape[0]), lambda i: (i, 0)),
            pl.BlockSpec((rows, fine), lambda i: (i, 0)),
            pl.BlockSpec((rows, fine), lambda i: (i, 0)),
            pl.BlockSpec((rows, 1), lambda i: (i, 0)),
        ],
        out_specs=pl.BlockSpec((2, rows, lon_total), lambda i: (0, i, 0)),
        out_shape=jax.ShapeDtypeStruct((2, count, lon_total), jnp.bfloat16),
    )(cos_a, sin_a, cos_b, sin_b, factor)


def all_reduce(value, axes):
    count = 1
    for name in axes:
        count *= lax.axis_size(name)
    flat = value.reshape(-1)
    chunk = -(-flat.shape[0] // (count * 128)) * 128
    flat = jnp.pad(flat, (0, chunk * count - flat.shape[0]))
    sent = flat.reshape(count, chunk).astype(jnp.bfloat16)
    parts = lax.all_to_all(sent, axes, 0, 0, tiled=True)
    owned = jnp.sum(parts.astype(jnp.float32), axis=0, keepdims=True)
    spread = jnp.broadcast_to(owned, (count, chunk))
    whole = lax.all_to_all(spread, axes, 0, 0, tiled=True).reshape(-1)
    return whole[: value.size].reshape(value.shape)


def masked_rows(ids_ref, pair_index, basis, rows_ref):
    half, length = basis.shape
    pair = ids_ref[pair_index]
    first = TRUNC + 1 - pair
    position = lax.broadcasted_iota(jnp.int32, (1, length), 1)
    lower = position < first
    upper = jnp.logical_and(position >= first, position < TRUNC + 2)
    offset = jnp.where(lower, position, position - first)
    odd = offset % 2 == 1
    zero = jnp.zeros_like(basis)
    signed = jnp.where(odd, -basis, basis)
    rows_ref[0:half, :] = jnp.where(lower, basis, zero)
    rows_ref[half : 2 * half, :] = jnp.where(lower, signed, zero)
    rows_ref[2 * half : 3 * half, :] = jnp.where(upper, basis, zero)
    rows_ref[3 * half : 4 * half, :] = jnp.where(upper, signed, zero)


def synth_kernel(ids_ref, spec_ref, basis_ref, out_ref, rows_ref):
    block = basis_ref.shape[0]
    step = pl.program_id(0)
    for i in range(block):
        masked_rows(ids_ref, step * block + i, basis_ref[i], rows_ref)
        out = lax.dot_general(
            rows_ref[...], spec_ref[i], (((1,), (1,)), ((), ())),
            preferred_element_type=jnp.float32,
        )
        out_ref[i] = out.astype(out_ref.dtype)


def analyse_kernel(ids_ref, grad_ref, basis_ref, out_ref, rows_ref):
    block = basis_ref.shape[0]
    step = pl.program_id(0)
    for i in range(block):
        masked_rows(ids_ref, step * block + i, basis_ref[i], rows_ref)
        out = lax.dot_general(
            grad_ref[i], rows_ref[...], (((0,), (0,)), ((), ())),
            preferred_element_type=jnp.float32,
        )
        out_ref[i] = out.astype(out_ref.dtype)


def pair_block(count):
    for size in (40, 20, 16, 8, 4, 2, 1):
        if count % size == 0:
            return size


def synthesis(local_ids, spectral, lat_basis):
    pairs, width, length = spectral.shape
    half = lat_basis.shape[1]
    block = pair_block(pairs)
    spec = pltpu.PrefetchScalarGridSpec(
        num_scalar_prefetch=1,
        grid=(pairs // block,),
        in_specs=[
            pl.BlockSpec((block, width, length), lambda s, ids: (s, 0, 0)),
            pl.BlockSpec((block, half, length), lambda s, ids: (s, 0, 0)),
        ],
        out_specs=pl.BlockSpec((block, 4 * half, width), lambda s, ids: (s, 0, 0)),
        scratch_shapes=[pltpu.VMEM((4 * half, length), lat_basis.dtype)],
    )
    return pl.pallas_call(
        synth_kernel,
        grid_spec=spec,
        out_shape=jax.ShapeDtypeStruct((pairs, 4 * half, width), jnp.bfloat16),
    )(local_ids, spectral, lat_basis)


def analysis(local_ids, grads, lat_basis):
    pairs, rows, width = grads.shape
    half, length = lat_basis.shape[1], lat_basis.shape[2]
    block = pair_block(pairs)
    spec = pltpu.PrefetchScalarGridSpec(
        num_scalar_prefetch=1,
        grid=(pairs // block,),
        in_specs=[
            pl.BlockSpec((block, rows, width), lambda s, ids: (s, 0, 0)),
            pl.BlockSpec((block, half, length), lambda s, ids: (s, 0, 0)),
        ],
        out_specs=pl.BlockSpec((block, width, length), lambda s, ids: (s, 0, 0)),
        scratch_shapes=[pltpu.VMEM((4 * half, length), lat_basis.dtype)],
    )
    return pl.pallas_call(
        analyse_kernel,
        grid_spec=spec,
        out_shape=jax.ShapeDtypeStruct((pairs, width, length), jnp.bfloat16),
    )(local_ids, grads, lat_basis)


def per_device(
    pair_table, spectral, lat_basis, in_weight, in_bias, out_weight, out_bias, cotangent
):
    pair_dev = spectral.shape[0]
    width_local = spectral.shape[1]
    lat_half = lat_basis.shape[1]
    band_rows = cotangent.shape[0]
    block_cols = cotangent.shape[2]
    lon_total = block_cols * lax.axis_size("lon")
    first_row = lax.axis_index("lat") * pair_dev
    local_ids = lax.dynamic_slice_in_dim(pair_table, first_row, pair_dev)
    lat_window = 2 * lat_half
    raw_waves = synthesis(local_ids, spectral, lat_basis).reshape(
        pair_dev, 2, lat_window, width_local
    )
    lat_index = jnp.arange(lat_window, dtype=jnp.int32)
    kernel_row = jnp.where(lat_index < lat_half, lat_index, 3 * lat_half - 1 - lat_index)
    reorder = (kernel_row[:, None] == lat_index[None, :]).astype(jnp.bfloat16)
    waves = jnp.einsum(
        "lr,pqrk->pqlk", reorder, raw_waves, preferred_element_type=jnp.float32
    ).astype(jnp.bfloat16)
    flat_waves = waves.reshape(2 * pair_dev, lat_window * width_local)
    band_waves = lax.all_to_all(flat_waves, "lat", split_axis=1, concat_axis=0, tiled=True)
    wave_count = band_waves.shape[0]
    coeff_grid = band_waves.reshape(wave_count, band_rows, width_local // 2, 2)
    numbers = wave_numbers(pair_table)
    full_table = fourier_table(numbers, lon_total)
    lon_parts = lax.axis_size("lon")
    block_table = full_table.reshape(2, wave_count, lon_parts, block_cols)
    all_columns = jnp.einsum(
        "glkc,cgbn->blkn", coeff_grid, block_table, preferred_element_type=jnp.float32
    ).astype(jnp.bfloat16)
    level_blocks = lax.all_to_all(all_columns, "lon", 0, 0, tiled=True)
    grid = jnp.swapaxes(level_blocks, 0, 1).reshape(band_rows, -1, block_cols)
    pre_act = (
        jnp.einsum("lkc,kh->lch", grid, in_weight, preferred_element_type=jnp.float32) + in_bias
    )
    activated, gelu_back = jax.vjp(jax.nn.gelu, pre_act)
    hidden = activated.astype(jnp.bfloat16)
    tendency = (
        jnp.einsum("lch,hk->lkc", hidden, out_weight, preferred_element_type=jnp.float32)
        + out_bias[None, :, None]
    ).astype(jnp.bfloat16)
    out_weight_part = jnp.einsum(
        "lch,lkc->kh", hidden, cotangent, preferred_element_type=jnp.float32
    )
    out_bias_part = jnp.sum(cotangent.astype(jnp.float32), axis=(0, 2))
    hidden_grad = jnp.einsum(
        "lkc,hk->lch", cotangent, out_weight, preferred_element_type=jnp.float32
    )
    pre_grad = gelu_back(hidden_grad)[0].astype(jnp.bfloat16)
    in_weight_part = jnp.einsum("lkc,lch->kh", grid, pre_grad, preferred_element_type=jnp.float32)
    in_bias_part = jnp.sum(pre_grad.astype(jnp.float32), axis=(0, 1))
    grid_grad = jnp.einsum(
        "lch,kh->lkc", pre_grad, in_weight, preferred_element_type=jnp.float32
    ).astype(jnp.bfloat16)
    channels, hid = in_weight.shape
    width = max(hid, channels)

    def widen(v):
        return jnp.pad(v, ((0, 0), (0, width - v.shape[1])))

    stacked = jnp.concatenate(
        [
            widen(in_weight_part),
            widen(out_weight_part),
            widen(in_bias_part[None, :]),
            widen(out_bias_part[None, :]),
        ],
        axis=0,
    )
    summed = all_reduce(stacked, ("lat", "lon"))
    in_weight_grad = summed[:channels, :hid]
    out_weight_grad = summed[channels : 2 * channels, :hid].T
    in_bias_grad = summed[2 * channels, :hid]
    out_bias_grad = summed[2 * channels + 1, :channels]
    grad_blocks = jnp.swapaxes(grid_grad.reshape(band_rows, lon_parts, -1, block_cols), 0, 1)
    level_rows = lax.all_to_all(grad_blocks, "lon", 0, 0, tiled=True)
    wave_grad = jnp.einsum(
        "cgbn,blkn->glkc", block_table, level_rows, preferred_element_type=jnp.float32
    ).astype(jnp.bfloat16)
    flat_grad = wave_grad.reshape(wave_count, band_rows * width_local)
    pair_grad = lax.all_to_all(flat_grad, "lat", split_axis=0, concat_axis=1, tiled=True)
    pair_grad = pair_grad.reshape(pair_dev, 2, lat_window, width_local)
    pair_grad = jnp.einsum(
        "lr,pqlk->pqrk", reorder, pair_grad, preferred_element_type=jnp.float32
    ).astype(jnp.bfloat16).reshape(pair_dev, 2 * lat_window, width_local)
    spectral_grad = analysis(local_ids, pair_grad, lat_basis)
    return (tendency, spectral_grad, in_weight_grad, in_bias_grad, out_weight_grad, out_bias_grad)


def solution(mesh):
    placed = (
        P(),
        P("lat", "lon", None),
        P("lat", None, None),
        P(),
        P(),
        P(),
        P(),
        P("lat", None, "lon"),
    )
    return jax.shard_map(
        per_device,
        mesh=mesh,
        in_specs=placed,
        out_specs=(P("lat", None, "lon"), P("lat", "lon", None), P(), P(), P(), P()),
        check_vma=False,
    )
```
